32 devices in a mesh: section: 2 (over core), shard: 4 (over z), replica: 4 (over y, x).
Axes of the slice: x: 2, y: 2, z: 4, core: 2. Of those that a mesh axis runs over, the one named last changes fastest.
Arguments:
- hidden_in: bfloat16 [2, 4, 256, 960], P(None, 'replica', 'shard'), may hold values from -6 to 6
- segment_ids: int32 [2, 4, 256], P(None, 'replica'), may hold values from 0 to 3, as said below
- norm_attn: bfloat16 [2, 960], P('section', 'shard'), may hold values from 0.099609375 to 1.8984375
- w_query: bfloat16 [2, 960, 960], P('section', 'shard'), may hold values from -0.1875 to 0.1875
- w_key: bfloat16 [2, 960, 320], P('section', 'shard'), may hold values from -0.1875 to 0.1875
- w_value: bfloat16 [2, 960, 320], P('section', 'shard'), may hold values from -0.1875 to 0.1875
- w_out: bfloat16 [2, 960, 960], P('section', 'shard'), may hold values from -0.75 to 0.75
- norm_ffn: bfloat16 [2, 960], P('section', 'shard'), may hold values from 0.099609375 to 1.8984375
- w_gate: bfloat16 [2, 960, 2560], P('section', 'shard'), may hold values from -0.1875 to 0.1875
- w_up: bfloat16 [2, 960, 2560], P('section', 'shard'), may hold values from -0.1875 to 0.1875
- w_down: bfloat16 [2, 2560, 960], P('section', 'shard'), may hold values from -0.125 to 0.125
- out_grad: bfloat16 [2, 4, 256, 960], P(None, 'replica', 'shard'), may hold values from -6 to 6
Outputs:
- layer_out: bfloat16 [2, 2, 4, 256, 960], P('section', None, 'replica', 'shard')
- input_grad: bfloat16 [2, 2, 4, 256, 960], P('section', None, 'replica', 'shard')
- grad_norm_attn: float32 [2, 960], P('section', 'shard')
- grad_w_query: float32 [2, 960, 960], P('section', 'shard')
- grad_w_key: float32 [2, 960, 320], P('section', 'shard')
- grad_w_value: float32 [2, 960, 320], P('section', 'shard')
- grad_w_out: float32 [2, 960, 960], P('section', 'shard')
- grad_norm_ffn: float32 [2, 960], P('section', 'shard')
- grad_w_gate: float32 [2, 960, 2560], P('section', 'shard')
- grad_w_up: float32 [2, 960, 2560], P('section', 'shard')
- grad_w_down: float32 [2, 2560, 960], P('section', 'shard')
The draws below stay inside these ranges and needn't reach their ends.
Inputs may be any that keep to these rules, and one draw needn't show every extreme that they name: `segment_ids`: along each sequence the segment numbers start at 0, never fall, and take every value up to the largest.
All inputs are finite; a program needn't handle non-finite values.
Results may differ from the reference program's by a relative error of at most 0.025.
Values may be sent and summed in bfloat16 or wider, within the bound.
No kernel may reach another device: no remote copies, remote signals or barrier semaphores. Data moves between devices by JAX's collectives and lax.ppermute only.
A program may use at most 192 MiB of HBM per device.

```python
import jax
import jax.numpy as jnp
from jax import lax

D = 960
QH = 15
KVH = 5
HD = 64
FF = 2560
QW = 960
KW = 320
GROUP = 64
MICRO = 2
SEQ = 256
BATCH = 4
LAYERS = 2


def draw_segment_ids(key, part):
    key_start, key_end, key_cut = jax.random.split(key, 3)
    draw_shape = (MICRO, BATCH, 1)
    first_end = jax.random.randint(key_start, draw_shape, 1, GROUP)
    long_end = jax.random.randint(key_end, draw_shape, SEQ - GROUP + 1, SEQ - 1)
    last_cut = jax.random.randint(key_cut, draw_shape, long_end + 1, SEQ)
    positions = jnp.arange(SEQ, dtype=jnp.int32)[None, None, :]
    return (positions >= first_end).astype(jnp.int32) + (positions >= long_end).astype(jnp.int32) + (positions >= last_cut).astype(jnp.int32)


def levels(own_key, shape, cuts, low, largest):
    def one(dim, shards_of):
        heights = jax.random.uniform(jax.random.fold_in(jax.random.fold_in(own_key, 6), dim), (shards_of,), jnp.float32, low / len(cuts), largest / len(cuts))
        return jnp.repeat(jnp.exp(heights), shape[dim] // shards_of).reshape((-1,) + (1,) * (len(shape) - dim - 1))

    loudness = one(*cuts[0])
    for cut in cuts[1:]:
        loudness = loudness * one(*cut)
    return loudness


def noise(stream_key, dims, width, limit, pieces=(), held_as=jnp.bfloat16):
    factor_of = levels(stream_key, dims, pieces, -0.22, 0.18) if pieces else 1.0
    values = jax.random.normal(stream_key, dims, jnp.float32) * width * factor_of
    return jnp.minimum(jnp.maximum(values, -limit), limit).astype(held_as)


def setup_inputs(seed: int = 0) -> dict:
    arg_keys = jax.random.split(jax.random.key(seed), 13)
    hidden_in = noise(arg_keys[0], (MICRO, BATCH, SEQ, D), 1.0, 6.0, ((1, 4), (2, 4)))
    segment_ids = draw_segment_ids(jax.random.fold_in(arg_keys[12], 71), 0)
    norm_attn = jnp.clip(1.0 + 0.18 * jax.random.normal(arg_keys[2], (LAYERS, D), jnp.float32), 0.099609375, 1.8984375).astype(jnp.bfloat16)
    w_query = noise(arg_keys[3], (LAYERS, D, QW), D ** -0.5, 0.1875, ((0, 2), (1, 4)))
    w_key = noise(arg_keys[4], (LAYERS, D, KW), D ** -0.5, 0.1875, ((0, 2), (1, 4)))
    w_value = noise(arg_keys[5], (LAYERS, D, KW), D ** -0.5, 0.1875, ((0, 2), (1, 4)))
    w_out = noise(arg_keys[6], (LAYERS, QW, D), (QW // 16) ** -0.5, 0.75, ((0, 2), (1, 4)))
    norm_ffn = jnp.clip(1.0 + 0.18 * jax.random.normal(arg_keys[7], (LAYERS, D), jnp.float32), 0.099609375, 1.8984375).astype(jnp.bfloat16)
    w_gate = noise(arg_keys[8], (LAYERS, D, FF), D ** -0.5, 0.1875, ((0, 2), (1, 4)))
    w_up = noise(arg_keys[9], (LAYERS, D, FF), D ** -0.5, 0.1875, ((0, 2), (1, 4)))
    w_down = noise(arg_keys[10], (LAYERS, FF, D), FF ** -0.5, 0.125, ((0, 2), (1, 4)))
    out_grad = noise(arg_keys[11], (MICRO, BATCH, SEQ, D), 1.0, 6.0, ((1, 4), (2, 4)))
    return {"hidden_in": hidden_in, "segment_ids": segment_ids, "norm_attn": norm_attn, "w_query": w_query, "w_key": w_key, "w_value": w_value, "w_out": w_out, "norm_ffn": norm_ffn, "w_gate": w_gate, "w_up": w_up, "w_down": w_down, "out_grad": out_grad}


rope_base = 100000.0
norm_eps = 1e-05
mask_fill = -1000000000.0
highest = lax.Precision.HIGHEST

@jax.custom_vjp
def low(v):
    return lax.optimization_barrier(v.astype(jnp.bfloat16)).astype(jnp.float32)

@jax.custom_vjp
def low_back(v):
    return v

def low_keep(v):
    return (low(v), None)

def low_pass(kept, grad):
    return (grad,)

def back_keep(v):
    return (v, None)

def back_low(kept, grad):
    return (low(grad),)
low.defvjp(low_keep, low_pass)
low_back.defvjp(back_keep, back_low)

def rotate_fwd(values, cos_tab, sin_tab):
    half_size = values.shape[-1] // 2
    turned = jnp.concatenate([-values[..., half_size:], values[..., :half_size]], axis=-1)
    return values * cos_tab + turned * sin_tab

def rope_tables(positions):
    frequency = rope_base ** (-jnp.arange(HD // 2).astype(jnp.float32) * (2.0 / HD))
    angles = positions.astype(jnp.float32)[..., None] * frequency
    angles = jnp.concatenate([angles, angles], axis=-1)
    return (jnp.cos(angles)[:, :, None, :], jnp.sin(angles)[:, :, None, :])

def doc_positions(segments):
    before = lax.optimization_barrier(jnp.sum((segments[:, None, :] < segments[:, :, None]).astype(jnp.int32), axis=-1))
    return jnp.arange(SEQ, dtype=jnp.int32)[None, :] - before

def attend(packed):
    queries, keys, values, segments = packed
    token_rows = jnp.arange(SEQ, dtype=jnp.int32)
    allowed = (segments[None, :] == segments[:, None]) & (token_rows[None, :] <= token_rows[:, None])
    query_heads = queries.reshape(SEQ, KVH, QH // KVH, HD)
    key_heads = keys.reshape(SEQ, KVH, HD)
    value_heads = values.reshape(SEQ, KVH, HD)
    scores = jnp.einsum('cgrd,sgd->grcs', query_heads, key_heads, precision=highest) * HD ** (-0.5)
    scores = low_back(jnp.where(allowed[None, None], scores, mask_fill))
    row_max = lax.optimization_barrier(jnp.max(scores, axis=-1, keepdims=True))
    exponent = jnp.exp(scores - row_max)
    prob_vals = exponent / lax.optimization_barrier(jnp.sum(exponent, axis=-1, keepdims=True))
    attended = jnp.einsum('grcs,sgd->cgrd', low(prob_vals), value_heads, precision=highest)
    return attended.reshape(SEQ, QH * HD)

def layer_ref(hidden, segments, params, cos_tab, sin_tab):
    gain_attn, query_w, key_w, value_w, out_w, gain_ffn, gate_w, up_w, down_w = params
    seq_count = hidden.shape[0]

    def project(left_rows, matrix):
        return jnp.einsum('nsd,de->nse', left_rows, matrix, precision=highest)
    scale_attn = lax.rsqrt(lax.optimization_barrier(jnp.mean(hidden * hidden, axis=-1, keepdims=True)) + norm_eps)
    normed = low(hidden * scale_attn * gain_attn)
    query_pre = low_back(project(normed, query_w)).reshape(seq_count, SEQ, QH, HD)
    queries = low(rotate_fwd(query_pre, cos_tab, sin_tab)).reshape(seq_count, SEQ, QH * HD)
    key_pre = low_back(project(normed, key_w)).reshape(seq_count, SEQ, KVH, HD)
    keys = low(rotate_fwd(key_pre, cos_tab, sin_tab)).reshape(seq_count, SEQ, KVH * HD)
    values = low(low_back(project(normed, value_w)))
    attended = lax.map(jax.checkpoint(attend), (queries, keys, values, segments))
    attended = low_back(low(attended))
    middle = hidden + low_back(project(attended, out_w))
    scale_ffn = lax.rsqrt(lax.optimization_barrier(jnp.mean(middle * middle, axis=-1, keepdims=True)) + norm_eps)
    normed_ffn = low(middle * scale_ffn * gain_ffn)
    gate_pre = low_back(project(normed_ffn, gate_w))
    up_pre = low_back(project(normed_ffn, up_w))
    hidden_act = low(jax.nn.silu(gate_pre) * up_pre)
    return middle + low_back(project(hidden_act, down_w))

def reference(hidden_in, segment_ids, norm_attn, w_query, w_key, w_value, w_out, norm_ffn, w_gate, w_up, w_down, out_grad):
    seq_count = MICRO * BATCH
    segments = segment_ids.reshape(seq_count, SEQ).astype(jnp.int32)
    cos_tab, sin_tab = rope_tables(doc_positions(segments))
    stacks = (norm_attn, w_query, w_key, w_value, w_out, norm_ffn, w_gate, w_up, w_down)
    layer_input = hidden_in.astype(jnp.float32).reshape(seq_count, SEQ, D)
    outputs = []
    backs = []
    for layer_num in range(LAYERS):
        params = tuple((stack_w[layer_num].astype(jnp.float32) for stack_w in stacks))
        if layer_num == 0:

            def run_layer(inputs, weights):
                return low(layer_ref(inputs, segments, weights, cos_tab, sin_tab))
        else:

            def run_layer(inputs, weights):
                return low(layer_ref(low_back(inputs), segments, weights, cos_tab, sin_tab))
        result, back_fn = jax.vjp(run_layer, layer_input, params)
        outputs.append(result)
        backs.append(back_fn)
        layer_input = result
    cotangent = out_grad.astype(jnp.float32).reshape(seq_count, SEQ, D)
    input_grads = [None] * LAYERS
    weight_grads = [None] * LAYERS
    for layer_num in reversed(range(LAYERS)):
        cotangent, weight_grads[layer_num] = backs[layer_num](cotangent)
        input_grads[layer_num] = cotangent
    full_shape = (LAYERS, MICRO, BATCH, SEQ, D)
    layer_out = jnp.stack(outputs).reshape(full_shape).astype(jnp.bfloat16)
    input_grad = jnp.stack(input_grads).reshape(full_shape).astype(jnp.bfloat16)
    grads = [jnp.stack([weight_grads[layer_num][which] for layer_num in range(LAYERS)]) for which in range(9)]
    return (layer_out, input_grad, grads[0], grads[1], grads[2], grads[3], grads[4], grads[5], grads[6], grads[7], grads[8])
```

```python
import jax
import jax.numpy as jnp
from jax import lax
from jax.sharding import PartitionSpec as P

QH = 15
KVH = 5
HD = 64
TEAM = 4

rope_base = 100000.0
norm_eps = 1e-05
mask_fill = -1000000000.0

low = jnp.bfloat16
wide = jnp.float32


def dot(a, b):
    return jnp.dot(a, b, preferred_element_type=wide)


def dot_t(a, b):
    return lax.dot_general(a, b, (((1,), (1,)), ((), ())), preferred_element_type=wide)


def dot_l(a, b):
    return lax.dot_general(a, b, (((0,), (0,)), ((), ())), preferred_element_type=wide)


def to_core(value, target):
    return lax.ppermute(value, "section", [(1 - target, target)])


def swap(value):
    return lax.ppermute(value, "section", [(0, 1), (1, 0)])


def z_send(value, hop, core=None):
    count = lax.axis_size("shard")
    cores = range(lax.axis_size("section")) if core is None else (core,)
    pairs = [(c * count + z, c * count + (z + hop) % count) for c in cores for z in range(count)]
    return lax.ppermute(value, ("section", "shard"), pairs)


def plane_send(value, flip, core=None):
    count = lax.axis_size("replica")
    cores = range(lax.axis_size("section")) if core is None else (core,)
    pairs = [(c * count + r, c * count + (r ^ flip)) for c in cores for r in range(count)]
    return lax.ppermute(value, ("section", "replica"), pairs)


def pick(stack, index):
    return lax.dynamic_index_in_dim(stack, index, 0, keepdims=False)


def place(parts):
    stack = jnp.zeros((len(parts),) + parts[0][1].shape, parts[0][1].dtype)
    for index, block in parts:
        stack = lax.dynamic_update_index_in_dim(stack, block, index, 0)
    return stack


def z_gather(block, z, core=None):
    return place([(z, block)] + [((z - hop) % 4, z_send(block, hop, core)) for hop in (1, 2, 3)])


def z_trade(stack, z, core=None):
    return [(z, pick(stack, z))] + [
        ((z - hop) % 4, z_send(pick(stack, (z + hop) % 4), hop, core)) for hop in (1, 2, 3)
    ]


def plane_gather(block, q, core=None):
    return place([(q, block)] + [(q ^ flip, plane_send(block, flip, core)) for flip in (1, 2, 3)])


def plane_trade(stack, q, core=None):
    return place(
        [(q, pick(stack, q))]
        + [(q ^ flip, plane_send(pick(stack, q ^ flip), flip, core)) for flip in (1, 2, 3)]
    )


def plane_sum(partial):
    half = partial.shape[0] // 2
    first, second = partial[:half].astype(low), partial[half:].astype(low)

    def both(mine, flip):
        return mine.astype(wide) + plane_send(mine, flip).astype(wide)

    first, second = both(first, 1).astype(low), both(second, 2).astype(low)
    return jnp.concatenate([both(first, 2), both(second, 1)])


def teams_sum(value):
    flip = TEAM
    while flip < lax.axis_size("replica"):
        sent = value.astype(low)
        value = sent.astype(wide) + plane_send(sent, flip).astype(wide)
        flip *= 2
    return value


def after(value, earlier):
    return lax.optimization_barrier((value, earlier))[0]


def tables(segments):
    count = segments.shape[0]
    rows = jnp.arange(count, dtype=jnp.int32)
    before = jnp.sum((segments[None, :] < segments[:, None]).astype(jnp.int32), axis=1)
    allowed = (segments[None, :] == segments[:, None]) & (rows[None, :] <= rows[:, None])
    frequency = rope_base ** (-jnp.arange(HD // 2).astype(wide) * (2.0 / HD))
    angles = (rows - before).astype(wide)[:, None] * frequency[None, :]
    angles = jnp.concatenate([angles, angles], axis=1)
    return allowed, jnp.cos(angles)[:, None, :], jnp.sin(angles)[:, None, :]


def rotate_fwd(values, cos_tab, sin_tab):
    half = HD // 2
    turned = jnp.concatenate([-values[..., half:], values[..., :half]], axis=-1)
    return values * cos_tab + turned * sin_tab


def rotate_back(values, cos_tab, sin_tab):
    half = HD // 2
    shifted = values * sin_tab
    return values * cos_tab + jnp.concatenate([shifted[..., half:], -shifted[..., :half]], axis=-1)


def row_scale(values):
    return lax.rsqrt(jnp.mean(values * values, axis=-1, keepdims=True) + norm_eps)


def norm_back(grad_normed, values, gain):
    factor = row_scale(values)
    gain_grad = jnp.sum(grad_normed * values * factor, axis=0)
    weighted = grad_normed * gain
    inner = jnp.mean(weighted * values, axis=-1, keepdims=True)
    return gain_grad, factor * weighted - values * factor * factor * factor * inner


def attention_fwd(layer_in, tabs, attn_w, gain):
    allowed, cos_tab, sin_tab = tabs
    count = layer_in.shape[0]
    x = layer_in.astype(wide)
    normed = (x * row_scale(x) * gain).astype(low)
    mixed = dot(normed, attn_w[1])
    query_pre = jnp.concatenate([dot(normed, attn_w[0]), mixed[:, :320]], axis=1)
    queries = rotate_fwd(query_pre.reshape(count, QH, HD), cos_tab, sin_tab).astype(low)
    queries = queries.reshape(count, KVH, QH // KVH, HD)
    keys = rotate_fwd(mixed[:, 320:].reshape(count, KVH, HD), cos_tab, sin_tab).astype(low)
    values = dot(normed, attn_w[2][:, :320]).astype(low).reshape(count, KVH, HD)
    scores = jnp.einsum("cgrd,sgd->grcs", queries, keys, preferred_element_type=wide) * HD**-0.5
    scores = jnp.where(allowed[None, None], scores, mask_fill)
    exponent = jnp.exp(scores - jnp.max(scores, axis=-1, keepdims=True))
    probs = exponent / jnp.sum(exponent, axis=-1, keepdims=True)
    attended = jnp.einsum("grcs,sgd->cgrd", probs.astype(low), values, preferred_element_type=wide)
    attended = attended.reshape(count, QH * HD).astype(low)
    branch = jnp.concatenate([dot(attended, attn_w[2][:, 320:]), dot(attended, attn_w[3])], axis=1)
    return x + branch, (normed, queries, keys, values, probs, attended)


def attention_back(layer_in, grad_middle, tabs, attn_w, gain, kept):
    allowed, cos_tab, sin_tab = tabs
    normed, queries, keys, values, probs, attended = kept
    count = layer_in.shape[0]
    branch = grad_middle.astype(low)
    grad_att = dot_t(branch[:, :320], attn_w[2][:, 320:]) + dot_t(branch[:, 320:], attn_w[3])
    grad_att = grad_att.astype(low).reshape(count, KVH, QH // KVH, HD)
    grad_probs = jnp.einsum("cgrd,sgd->grcs", grad_att, values, preferred_element_type=wide)
    centre = jnp.sum(probs * grad_probs, axis=-1, keepdims=True)
    grad_scores = (probs * (grad_probs - centre)).astype(low)
    scale = HD**-0.5
    grad_q = jnp.einsum("grcs,sgd->cgrd", grad_scores, keys, preferred_element_type=wide) * scale
    grad_k = jnp.einsum("grcs,cgrd->sgd", grad_scores, queries, preferred_element_type=wide) * scale
    grad_v = jnp.einsum(
        "grcs,cgrd->sgd", probs.astype(low), grad_att, preferred_element_type=wide
    )
    grad_q = rotate_back(grad_q.reshape(count, QH, HD), cos_tab, sin_tab).astype(low)
    grad_k = rotate_back(grad_k, cos_tab, sin_tab).astype(low)
    pieces = [
        grad_q.reshape(count, QH * HD),
        grad_k.reshape(count, KVH * HD),
        grad_v.astype(low).reshape(count, KVH * HD),
        branch,
    ]
    right = jnp.concatenate(pieces, axis=1)
    grad_normed = (
        dot_t(right[:, :640], attn_w[0])
        + dot_t(right[:, 640:1280], attn_w[1])
        + dot_t(right[:, 1280:1600], attn_w[2][:, :320])
    )
    x = layer_in.astype(wide)
    gain_grad, through = norm_back(grad_normed, x, gain)
    return grad_middle + through, right, gain_grad


def local(
    hidden_in,
    segment_ids,
    norm_attn,
    w_query,
    w_key,
    w_value,
    w_out,
    norm_ffn,
    w_gate,
    w_up,
    w_down,
    out_grad,
):
    core = lax.axis_index("section")
    z = lax.axis_index("shard")
    replica = lax.axis_index("replica")
    q = replica % TEAM
    layers = 2
    group, width = hidden_in.shape[2], hidden_in.shape[3]

    chunk = (w_query.shape[2] * 2 + w_key.shape[2] * 2) // TEAM
    hid = w_gate.shape[2] // TEAM
    down_rows = w_down.shape[1] // TEAM
    attn_all = jnp.concatenate([w_query[0], w_key[0], w_value[0], w_out[0]], axis=1)
    attn_share = lax.dynamic_slice_in_dim(attn_all, q * chunk, chunk, axis=1)
    ffn_share = jnp.concatenate(
        [
            lax.dynamic_slice_in_dim(w_gate[0], q * hid, hid, axis=1),
            lax.dynamic_slice_in_dim(w_up[0], q * hid, hid, axis=1),
        ],
        axis=1,
    )
    down_share = lax.dynamic_slice_in_dim(w_down[0], q * down_rows, down_rows, axis=0)

    def give(value, owner):
        return jnp.where(core == owner, value, to_core(value, 1 - owner))

    def load_attn(owner, share):
        rows = z_gather(share, z, owner).reshape(-1, chunk)
        return give(plane_gather(rows, q, owner), owner)

    def load_ffn(owner, share):
        return give(z_gather(share, z, owner).reshape(-1, 2 * hid), owner)

    def load_down(owner, share):
        blocks = plane_trade(z_gather(share, z, owner), q, owner)
        return give(blocks.reshape(-1, width), owner)

    def whole_sequence(shares):
        mine = pick(shares[:, 0], core)
        blocks = plane_gather(mine, q)
        return place(z_trade(blocks, z)).reshape(-1, width)

    hidden = whole_sequence(hidden_in)
    segments = pick(plane_gather(pick(segment_ids[:, 0], core), q), z)
    tabs = tables(segments)
    own_gains = jnp.concatenate([norm_attn, norm_ffn], axis=0)
    own_gains = z_gather(own_gains, z).transpose(1, 0, 2).reshape(2, -1).astype(wide)
    other_gains = swap(own_gains.astype(low)).astype(wide)
    gains = [jnp.where(core == layer, own_gains, other_gains) for layer in range(layers)]

    attn_w, ffn_w, down_w = [None] * 2, [None] * 2, [None] * 2
    attn_w[0] = load_attn(0, attn_share)
    ffn_w[0] = load_ffn(0, ffn_share)
    down_w[0] = load_down(0, down_share)
    attn_w[1] = load_attn(1, after(attn_share, attn_w[0]))
    ffn_w[1] = load_ffn(1, after(ffn_share, ffn_w[0]))
    down_w[1] = load_down(1, after(down_share, down_w[0]))
    top_grad = whole_sequence(after(out_grad, attn_w[0]))

    inputs, kept, outputs = [hidden], [], []
    for layer in range(layers):
        middle, kept_attn = attention_fwd(inputs[layer], tabs, attn_w[layer], gains[layer][0])
        normed = (middle * row_scale(middle) * gains[layer][1]).astype(low)
        both = dot(normed, ffn_w[layer])
        gate, up = both[:, :hid], both[:, hid:]
        act = (gate * jax.nn.sigmoid(gate) * up).astype(low)
        kept.append((kept_attn, middle, normed, gate, up, act))
        result = (middle + plane_sum(dot(act, down_w[layer]))).astype(low)
        outputs.append(result)
        inputs.append(result)

    gain_grads, input_grads, sums = [None] * 2, [None] * 2, [None] * 2
    grad = top_grad
    for layer in reversed(range(layers)):
        kept_attn, middle, normed, gate, up, act = kept[layer]
        grad_act = dot_t(grad, down_w[layer])
        sig = jax.nn.sigmoid(gate)
        grad_gate = (grad_act * up * sig * (1.0 + gate * (1.0 - sig))).astype(low)
        grad_up = (grad_act * gate * sig).astype(low)
        grad_both = jnp.concatenate([grad_gate, grad_up], axis=1)
        grad_normed = plane_sum(dot_t(grad_both, ffn_w[layer]))
        gain_ffn, through = norm_back(grad_normed, middle, gains[layer][1])
        grad_middle = grad.astype(wide) + through
        grad_in, right, gain_attn = attention_back(
            inputs[layer], grad_middle, tabs, attn_w[layer], gains[layer][0], kept_attn
        )
        gain_grads[layer] = jnp.stack([gain_attn, gain_ffn])

        def collect(partial):
            return partial + to_core(partial.astype(low), layer).astype(wide)

        def along_z(stack):
            blocks = z_trade(stack.astype(low), z, layer)
            total = sum(block.astype(wide) for _, block in blocks)
            return plane_gather(teams_sum(total).astype(low), q, layer)

        ffn_sum = along_z(collect(dot_l(normed, grad_both)).reshape(4, -1, 2 * hid))
        down_part = collect(dot_l(act, grad)).astype(low).reshape(TEAM, down_rows, width)
        down_sum = along_z(plane_trade(down_part, q, layer))
        own_right = lax.dynamic_slice_in_dim(right, q * chunk, chunk, axis=1)
        split = w_query.shape[2] + w_key.shape[2] * 2
        column = q * chunk + jnp.arange(chunk)
        attn_part = jnp.where(
            column[None, :] < split,
            dot_l(kept_attn[0], own_right),
            dot_l(kept_attn[5], own_right),
        )
        attn_sum = along_z(collect(attn_part).reshape(4, -1, chunk))
        sums[layer] = (attn_sum, ffn_sum, down_sum)
        grad = grad_in.astype(low)
        input_grads[layer] = grad

    def spread(by_layer):
        mine = jnp.where(core == 0, by_layer[0], by_layer[1])
        other = swap(jnp.where(core == 0, by_layer[1], by_layer[0]))
        stack = jnp.where(
            core == 0, jnp.stack([mine, other]), jnp.stack([other, mine])
        ).reshape(2, 4, group, width)
        replicas = lax.axis_size("replica")

        def slice_for(target):
            return lax.dynamic_index_in_dim(stack, target, 1, keepdims=False)

        total = jnp.where(z == q, slice_for(z), 0)
        for hop in (1, 2, 3):
            pairs = [
                ((r % TEAM) * replicas + r, (r % TEAM + hop) % 4 * replicas + r)
                for r in range(replicas)
            ]
            total = total + lax.ppermute(slice_for((z + hop) % 4), ("shard", "replica"), pairs)
        return total[None, :, None]

    layer_out = spread(outputs)
    input_grad = spread(input_grads)

    gain_all = jnp.stack(gain_grads)
    gain_all = gain_all + swap(gain_all)
    total = gain_all
    for hop in (1, 2, 3):
        total = total + z_send(gain_all, hop)
    flip = TEAM
    while flip < lax.axis_size("replica"):
        total = total + plane_send(total, flip)
        flip *= 2
    total = jnp.where(core == 0, total[0], total[1])
    total = lax.dynamic_index_in_dim(total.reshape(2, 4, -1), z, 1, keepdims=False)

    attn_sum, ffn_sum, down_sum = (
        jnp.where(core == 0, first, second).astype(wide) for first, second in zip(*sums)
    )
    attn_cols = jnp.concatenate([attn_sum[chunk_num] for chunk_num in range(TEAM)], axis=1)
    qw, kw = w_query.shape[2], w_key.shape[2]
    gate_cols = jnp.concatenate([ffn_sum[num, :, :hid] for num in range(TEAM)], axis=1)
    up_cols = jnp.concatenate([ffn_sum[num, :, hid:] for num in range(TEAM)], axis=1)
    return (
        layer_out,
        input_grad,
        total[0][None],
        attn_cols[None, :, :qw],
        attn_cols[None, :, qw : qw + kw],
        attn_cols[None, :, qw + kw : qw + 2 * kw],
        attn_cols[None, :, qw + 2 * kw :],
        total[1][None],
        gate_cols[None],
        up_cols[None],
        down_sum.reshape(1, -1, width),
    )


def solution(mesh):
    placed = (
        P(None, "replica", "shard", None),
        P(None, "replica", None),
        P("section", "shard"),
        P("section", "shard", None),
        P("section", "shard", None),
        P("section", "shard", None),
        P("section", "shard", None),
        P("section", "shard"),
        P("section", "shard", None),
        P("section", "shard", None),
        P("section", "shard", None),
        P(None, "replica", "shard", None),
    )
    return jax.shard_map(
        local,
        mesh=mesh,
        in_specs=placed,
        out_specs=(
            P("section", None, "replica", "shard", None),
            P("section", None, "replica", "shard", None),
            P("section", "shard"),
            P("section", "shard", None),
            P("section", "shard", None),
            P("section", "shard", None),
            P("section", "shard", None),
            P("section", "shard"),
            P("section", "shard", None),
            P("section", "shard", None),
            P("section", "shard", None),
        ),
        check_vma=False,
    )
```

```python
import jax
import jax.numpy as jnp
from jax import lax
from jax.sharding import PartitionSpec as P

QH = 15
KVH = 5
HD = 64
TEAM = 4

rope_base = 100000.0
norm_eps = 1e-05
mask_fill = -1000000000.0

low = jnp.bfloat16
wide = jnp.float32


def dot(a, b):
    return jnp.dot(a, b, preferred_element_type=wide)


def dot_t(a, b):
    return lax.dot_general(a, b, (((1,), (1,)), ((), ())), preferred_element_type=wide)


def dot_l(a, b):
    return lax.dot_general(a, b, (((0,), (0,)), ((), ())), preferred_element_type=wide)


def to_core(value, target):
    return lax.ppermute(value, "section", [(1 - target, target)])


def swap(value):
    return lax.ppermute(value, "section", [(0, 1), (1, 0)])


def z_send(value, hop, core=None):
    count = lax.axis_size("shard")
    cores = range(lax.axis_size("section")) if core is None else (core,)
    pairs = [(c * count + z, c * count + (z + hop) % count) for c in cores for z in range(count)]
    return lax.ppermute(value, ("section", "shard"), pairs)


def plane_send(value, flip, core=None):
    count = lax.axis_size("replica")
    cores = range(lax.axis_size("section")) if core is None else (core,)
    pairs = [(c * count + r, c * count + (r ^ flip)) for c in cores for r in range(count)]
    return lax.ppermute(value, ("section", "replica"), pairs)


def pick(stack, index):
    return lax.dynamic_index_in_dim(stack, index, 0, keepdims=False)


def place(parts):
    stack = jnp.zeros((len(parts),) + parts[0][1].shape, parts[0][1].dtype)
    for index, block in parts:
        stack = lax.dynamic_update_index_in_dim(stack, block, index, 0)
    return stack


def z_gather(block, z, core=None):
    return place([(z, block)] + [((z - hop) % 4, z_send(block, hop, core)) for hop in (1, 2, 3)])


def z_trade(stack, z, core=None):
    return [(z, pick(stack, z))] + [
        ((z - hop) % 4, z_send(pick(stack, (z + hop) % 4), hop, core)) for hop in (1, 2, 3)
    ]


def plane_gather(block, q, core=None):
    return place([(q, block)] + [(q ^ flip, plane_send(block, flip, core)) for flip in (1, 2, 3)])


def plane_trade(stack, q, core=None):
    return place(
        [(q, pick(stack, q))]
        + [(q ^ flip, plane_send(pick(stack, q ^ flip), flip, core)) for flip in (1, 2, 3)]
    )


def plane_sum(partial):
    half = partial.shape[0] // 2
    first, second = partial[:half].astype(low), partial[half:].astype(low)

    def both(mine, flip):
        return mine.astype(wide) + plane_send(mine, flip).astype(wide)

    first, second = both(first, 1).astype(low), both(second, 2).astype(low)
    return jnp.concatenate([both(first, 2), both(second, 1)])


def teams_sum(value):
    flip = TEAM
    while flip < lax.axis_size("replica"):
        sent = value.astype(low)
        value = sent.astype(wide) + plane_send(sent, flip).astype(wide)
        flip *= 2
    return value


def after(value, earlier):
    return lax.optimization_barrier((value, earlier))[0]


def fold(block, width):
    rows, cols = block.shape[-2], block.shape[-1]
    if cols % width == 0:
        return jnp.concatenate(
            [block[..., start : start + width] for start in range(0, cols, width)], axis=-2
        )
    tail = block[..., width:]
    tail = jnp.concatenate([tail[..., : rows // 2, :], tail[..., rows // 2 :, :]], axis=-1)
    return jnp.concatenate([block[..., :width], tail], axis=-2)


def unfold(block, cols):
    width = block.shape[-1]
    if cols % width == 0:
        rows = block.shape[-2] * width // cols
        return jnp.concatenate(
            [block[..., k * rows : (k + 1) * rows, :] for k in range(cols // width)], axis=-1
        )
    rows = block.shape[-2] * width // cols
    tail = block[..., rows:, :]
    tail = jnp.concatenate([tail[..., : width // 2], tail[..., width // 2 :]], axis=-2)
    return jnp.concatenate([block[..., :rows, :], tail], axis=-1)


def tables(segments):
    count = segments.shape[0]
    rows = jnp.arange(count, dtype=jnp.int32)
    before = jnp.sum((segments[None, :] < segments[:, None]).astype(jnp.int32), axis=1)
    allowed = (segments[None, :] == segments[:, None]) & (rows[None, :] <= rows[:, None])
    frequency = rope_base ** (-jnp.arange(HD // 2).astype(wide) * (2.0 / HD))
    angles = (rows - before).astype(wide)[:, None] * frequency[None, :]
    angles = jnp.concatenate([angles, angles], axis=1)
    return allowed, jnp.cos(angles)[:, None, :], jnp.sin(angles)[:, None, :]


def rotate_fwd(values, cos_tab, sin_tab):
    half = HD // 2
    turned = jnp.concatenate([-values[..., half:], values[..., :half]], axis=-1)
    return values * cos_tab + turned * sin_tab


def rotate_back(values, cos_tab, sin_tab):
    half = HD // 2
    shifted = values * sin_tab
    return values * cos_tab + jnp.concatenate([shifted[..., half:], -shifted[..., :half]], axis=-1)


def row_scale(values):
    return lax.rsqrt(jnp.mean(values * values, axis=-1, keepdims=True) + norm_eps)


def norm_back(grad_normed, values, gain):
    factor = row_scale(values)
    gain_grad = jnp.sum(grad_normed * values * factor, axis=0)
    weighted = grad_normed * gain
    inner = jnp.mean(weighted * values, axis=-1, keepdims=True)
    return gain_grad, factor * weighted - values * factor * factor * factor * inner


def attention_fwd(layer_in, tabs, attn_w, gain):
    allowed, cos_tab, sin_tab = tabs
    count = layer_in.shape[0]
    x = layer_in.astype(wide)
    normed = (x * row_scale(x) * gain).astype(low)
    mixed = dot(normed, attn_w[1])
    query_pre = jnp.concatenate([dot(normed, attn_w[0]), mixed[:, :320]], axis=1)
    queries = rotate_fwd(query_pre.reshape(count, QH, HD), cos_tab, sin_tab).astype(low)
    queries = queries.reshape(count, KVH, QH // KVH, HD)
    keys = rotate_fwd(mixed[:, 320:].reshape(count, KVH, HD), cos_tab, sin_tab).astype(low)
    values = dot(normed, attn_w[2][:, :320]).astype(low).reshape(count, KVH, HD)
    scores = jnp.einsum("cgrd,sgd->grcs", queries, keys, preferred_element_type=wide) * HD**-0.5
    scores = jnp.where(allowed[None, None], scores, mask_fill)
    exponent = jnp.exp(scores - jnp.max(scores, axis=-1, keepdims=True))
    probs = exponent / jnp.sum(exponent, axis=-1, keepdims=True)
    attended = jnp.einsum("grcs,sgd->cgrd", probs.astype(low), values, preferred_element_type=wide)
    attended = attended.reshape(count, QH * HD).astype(low)
    branch = jnp.concatenate([dot(attended, attn_w[2][:, 320:]), dot(attended, attn_w[3])], axis=1)
    return x + branch, (normed, queries, keys, values, probs, attended)


def attention_back(layer_in, grad_middle, tabs, attn_w, gain, kept):
    allowed, cos_tab, sin_tab = tabs
    normed, queries, keys, values, probs, attended = kept
    count = layer_in.shape[0]
    branch = grad_middle.astype(low)
    grad_att = dot_t(branch[:, :320], attn_w[2][:, 320:]) + dot_t(branch[:, 320:], attn_w[3])
    grad_att = grad_att.astype(low).reshape(count, KVH, QH // KVH, HD)
    grad_probs = jnp.einsum("cgrd,sgd->grcs", grad_att, values, preferred_element_type=wide)
    centre = jnp.sum(probs * grad_probs, axis=-1, keepdims=True)
    grad_scores = (probs * (grad_probs - centre)).astype(low)
    scale = HD**-0.5
    grad_q = jnp.einsum("grcs,sgd->cgrd", grad_scores, keys, preferred_element_type=wide) * scale
    grad_k = jnp.einsum("grcs,cgrd->sgd", grad_scores, queries, preferred_element_type=wide) * scale
    grad_v = jnp.einsum(
        "grcs,cgrd->sgd", probs.astype(low), grad_att, preferred_element_type=wide
    )
    grad_q = rotate_back(grad_q.reshape(count, QH, HD), cos_tab, sin_tab).astype(low)
    grad_k = rotate_back(grad_k, cos_tab, sin_tab).astype(low)
    pieces = [
        grad_q.reshape(count, QH * HD),
        grad_k.reshape(count, KVH * HD),
        grad_v.astype(low).reshape(count, KVH * HD),
        branch,
    ]
    right = jnp.concatenate(pieces, axis=1)
    grad_normed = (
        dot_t(right[:, :640], attn_w[0])
        + dot_t(right[:, 640:1280], attn_w[1])
        + dot_t(right[:, 1280:1600], attn_w[2][:, :320])
    )
    x = layer_in.astype(wide)
    gain_grad, through = norm_back(grad_normed, x, gain)
    return grad_middle + through, right, gain_grad


def local(
    hidden_in,
    segment_ids,
    norm_attn,
    w_query,
    w_key,
    w_value,
    w_out,
    norm_ffn,
    w_gate,
    w_up,
    w_down,
    out_grad,
):
    core = lax.axis_index("section")
    z = lax.axis_index("shard")
    replica = lax.axis_index("replica")
    q = replica % TEAM
    layers = 2
    group, width = hidden_in.shape[2], hidden_in.shape[3]

    chunk = (w_query.shape[2] * 2 + w_key.shape[2] * 2) // TEAM
    hid = w_gate.shape[2] // TEAM
    down_rows = w_down.shape[1] // TEAM
    attn_all = jnp.concatenate([w_query[0], w_key[0], w_value[0], w_out[0]], axis=1)
    attn_share = lax.dynamic_slice_in_dim(attn_all, q * chunk, chunk, axis=1)
    ffn_share = jnp.concatenate(
        [
            lax.dynamic_slice_in_dim(w_gate[0], q * hid, hid, axis=1),
            lax.dynamic_slice_in_dim(w_up[0], q * hid, hid, axis=1),
        ],
        axis=1,
    )
    down_share = lax.dynamic_slice_in_dim(w_down[0], q * down_rows, down_rows, axis=0)

    def give(value, owner):
        return jnp.where(core == owner, value, to_core(value, 1 - owner))

    def both_layers(own):
        other = swap(own)
        return [jnp.where(core == layer, own, other) for layer in range(layers)]

    def whole_sequence(mine):
        blocks = plane_gather(mine, q)
        return lax.all_to_all(blocks, "shard", 0, 0, tiled=False)

    attn_rows = z_gather(attn_share, z, 0).reshape(-1, chunk)
    turn = to_core(attn_rows[:16, :128], 1)
    own_segments = lax.dynamic_slice_in_dim(pick(segment_ids[:, 0], core), z * group, group)
    marks = jnp.zeros((16, width), low).at[0, :group].set(own_segments.astype(low))
    entry = whole_sequence(jnp.concatenate([pick(hidden_in[:, 0], core), marks]))
    hidden = entry[:, :group].reshape(-1, width)
    segments = entry[:, group, :group].reshape(-1).astype(jnp.int32)
    tabs = tables(segments)

    own_gains = lax.all_gather(jnp.concatenate([norm_attn, norm_ffn]), "shard")
    gains = both_layers(own_gains.transpose(1, 0, 2).reshape(2, -1))
    gains = [gain.astype(wide) for gain in gains]

    ffn_pair = jnp.concatenate([ffn_share, fold(down_share, chunk)], axis=1)
    ffn_pair = lax.all_gather(ffn_pair, "shard")

    attn_w = [None] * 2
    attn_w[0] = give(plane_gather(attn_rows, q, 0), 0)
    rows = z_gather(after(attn_share, turn), z, 1).reshape(-1, chunk)
    attn_w[1] = give(plane_gather(after(rows, attn_w[0]), q, 1), 1)
    ffn_w = both_layers(ffn_pair[:, :, : 2 * hid].reshape(-1, 2 * hid))
    down_w = both_layers(
        unfold(plane_trade(ffn_pair[:, :, 2 * hid :], q), width).reshape(-1, width)
    )
    top_grad = whole_sequence(pick(after(out_grad, attn_w[1])[:, 0], core)).reshape(-1, width)

    inputs, kept, outputs = [hidden], [], []
    for layer in range(layers):
        middle, kept_attn = attention_fwd(inputs[layer], tabs, attn_w[layer], gains[layer][0])
        normed = (middle * row_scale(middle) * gains[layer][1]).astype(low)
        both = dot(normed, ffn_w[layer])
        gate, up = both[:, :hid], both[:, hid:]
        act = (gate * jax.nn.sigmoid(gate) * up).astype(low)
        kept.append((kept_attn, middle, normed, gate, up, act))
        result = (middle + plane_sum(dot(act, down_w[layer]))).astype(low)
        if layer == 0:
            result, top_grad = lax.optimization_barrier((result, top_grad))
        outputs.append(result)
        inputs.append(result)

    def spread(by_layer):
        mine = jnp.where(core == 0, by_layer[0], by_layer[1])
        other = swap(jnp.where(core == 0, by_layer[1], by_layer[0]))
        stack = jnp.where(
            core == 0, jnp.stack([mine, other]), jnp.stack([other, mine])
        ).reshape(2, 4, group, width)
        replicas = lax.axis_size("replica")

        def slice_for(target):
            return lax.dynamic_index_in_dim(stack, target, 1, keepdims=False)

        total = jnp.where(z == q, slice_for(z), 0)
        for hop in (1, 2, 3):
            pairs = [
                ((r % TEAM) * replicas + r, (r % TEAM + hop) % 4 * replicas + r)
                for r in range(replicas)
            ]
            total = total + lax.ppermute(slice_for((z + hop) % 4), ("shard", "replica"), pairs)
        return total[None, :, None]

    def exchange(mine, other):
        return (mine + swap(other.astype(low)).astype(wide)).astype(low)

    def halves(value):
        first, second = value
        return jnp.where(core == 0, first, second), jnp.where(core == 0, second, first)

    def sum_z(stack):
        total = lax.psum_scatter(stack, "shard", scatter_dimension=0, tiled=False)
        return teams_sum(total.astype(wide)).astype(low)

    half = chunk // 2
    split = w_query.shape[2] + w_key.shape[2] * 2

    def attn_half(kept_attn, right, which):
        start = q * chunk + which * half
        part = lax.dynamic_slice_in_dim(right, start, half, axis=1)
        column = start + jnp.arange(half)
        return jnp.where(
            column[None, :] < split, dot_l(kept_attn[0], part), dot_l(kept_attn[5], part)
        )

    gain_grads, input_grads = [None] * 2, [None] * 2
    attn_sums, pair_sums = [None] * 2, [None] * 2
    grad = top_grad
    for layer in reversed(range(layers)):
        kept_attn, middle, normed, gate, up, act = kept[layer]
        grad_act = dot_t(grad, down_w[layer])
        sig = jax.nn.sigmoid(gate)
        grad_gate = (grad_act * up * sig * (1.0 + gate * (1.0 - sig))).astype(low)
        grad_up = (grad_act * gate * sig).astype(low)
        grad_both = jnp.concatenate([grad_gate, grad_up], axis=1)
        grad_normed = plane_sum(dot_t(grad_both, ffn_w[layer]))

        mine, other = halves((grad_gate, grad_up))
        ffn_part = exchange(dot_l(normed, mine), dot_l(normed, other))
        step = down_rows // 2
        strips = [
            jnp.concatenate(
                [act[:, k * down_rows + c * step :][:, :step] for k in range(TEAM)], axis=1
            )
            for c in (0, 1)
        ]
        mine, other = halves(strips)
        down_part = exchange(dot_l(mine, grad), dot_l(other, grad))
        grad_normed, ffn_part, down_part = lax.optimization_barrier(
            (grad_normed, ffn_part, down_part)
        )
        down_part = plane_trade(down_part.reshape(TEAM, step, width), q)
        gain_ffn, through = norm_back(grad_normed, middle, gains[layer][1])
        grad_middle = grad.astype(wide) + through
        grad_in, right, gain_attn = attention_back(
            inputs[layer], grad_middle, tabs, attn_w[layer], gains[layer][0], kept_attn
        )
        grad = grad_in.astype(low)
        grad, down_part = lax.optimization_barrier((grad, down_part))
        pair = jnp.concatenate(
            [ffn_part.reshape(4, -1, hid), fold(down_part, half)], axis=2
        )
        pair_sums[layer] = sum_z(pair)
        attn_part = exchange(
            attn_half(kept_attn, right, core), attn_half(kept_attn, right, 1 - core)
        )
        attn_sums[layer] = sum_z(attn_part.reshape(4, -1, half))
        gain_grads[layer] = jnp.stack([gain_attn, gain_ffn])
        input_grads[layer] = grad
        if layer == 1:
            layer_out = spread(outputs)

    input_grad = spread(input_grads)
    whole_1 = plane_gather(jnp.concatenate([pair_sums[1], attn_sums[1]], axis=1), q)
    whole_0 = jnp.concatenate(
        [plane_gather(pair_sums[0], q), plane_gather(attn_sums[0], q)], axis=2
    )
    own = jnp.where(core == 0, whole_0, whole_1)
    other = swap(jnp.where(core == 0, whole_1, whole_0))
    by_half = (jnp.where(core == 0, own, other), jnp.where(core == 0, other, own))

    gain_all = jnp.stack(gain_grads)
    gain_all = gain_all + swap(gain_all)
    total = gain_all
    for hop in (1, 2, 3):
        total = total + z_send(gain_all, hop)
    flip = TEAM
    while flip < lax.axis_size("replica"):
        total = total + plane_send(total, flip)
        flip *= 2
    total = jnp.where(core == 0, total[0], total[1])
    total = lax.dynamic_index_in_dim(total.reshape(2, 4, -1), z, 1, keepdims=False)

    attn_cols = jnp.concatenate(
        [part[num, :, hid + half :] for num in range(TEAM) for part in by_half], axis=1
    ).astype(wide)
    gate_cols, up_cols = (
        jnp.concatenate([part[num, :, :hid] for num in range(TEAM)], axis=1).astype(wide)
        for part in by_half
    )
    down_sum = jnp.stack(
        [unfold(part[:, :, hid : hid + half], width) for part in by_half], axis=1
    ).astype(wide)
    qw, kw = w_query.shape[2], w_key.shape[2]
    return (
        layer_out,
        input_grad,
        total[0][None],
        attn_cols[None, :, :qw],
        attn_cols[None, :, qw : qw + kw],
        attn_cols[None, :, qw + kw : qw + 2 * kw],
        attn_cols[None, :, qw + 2 * kw :],
        total[1][None],
        gate_cols[None],
        up_cols[None],
        down_sum.reshape(1, -1, width),
    )


def solution(mesh):
    placed = (
        P(None, "replica", "shard", None),
        P(None, "replica", None),
        P("section", "shard"),
        P("section", "shard", None),
        P("section", "shard", None),
        P("section", "shard", None),
        P("section", "shard", None),
        P("section", "shard"),
        P("section", "shard", None),
        P("section", "shard", None),
        P("section", "shard", None),
        P(None, "replica", "shard", None),
    )
    return jax.shard_map(
        local,
        mesh=mesh,
        in_specs=placed,
        out_specs=(
            P("section", None, "replica", "shard", None),
            P("section", None, "replica", "shard", None),
            P("section", "shard"),
            P("section", "shard", None),
            P("section", "shard", None),
            P("section", "shard", None),
            P("section", "shard", None),
            P("section", "shard"),
            P("section", "shard", None),
            P("section", "shard", None),
            P("section", "shard", None),
        ),
        check_vma=False,
    )
```

```python
import jax
import jax.numpy as jnp
from jax import lax
from jax.experimental import pallas as pl
from jax.experimental.pallas import tpu as pltpu
from jax.sharding import PartitionSpec as P

QH = 15
KVH = 5
HD = 64
TEAM = 4

rope_base = 100000.0
norm_eps = 1e-05
mask_fill = -1000000000.0

low = jnp.bfloat16
wide = jnp.float32


def dot(a, b):
    return jnp.dot(a, b, preferred_element_type=wide)


def dot_t(a, b):
    return lax.dot_general(a, b, (((1,), (1,)), ((), ())), preferred_element_type=wide)


def dot_l(a, b):
    return lax.dot_general(a, b, (((0,), (0,)), ((), ())), preferred_element_type=wide)


def to_core(value, target):
    return lax.ppermute(value, "section", [(1 - target, target)])


def swap(value):
    return lax.ppermute(value, "section", [(0, 1), (1, 0)])


def z_send(value, hop, core=None):
    count = lax.axis_size("shard")
    cores = range(lax.axis_size("section")) if core is None else (core,)
    pairs = [(c * count + z, c * count + (z + hop) % count) for c in cores for z in range(count)]
    return lax.ppermute(value, ("section", "shard"), pairs)


def plane_send(value, flip, core=None):
    count = lax.axis_size("replica")
    cores = range(lax.axis_size("section")) if core is None else (core,)
    pairs = [(c * count + r, c * count + (r ^ flip)) for c in cores for r in range(count)]
    return lax.ppermute(value, ("section", "replica"), pairs)


def pick(stack, index):
    return lax.dynamic_index_in_dim(stack, index, 0, keepdims=False)


def place_kernel(index_ref, *refs):
    *blocks, stack, sems = refs
    copies = [
        pltpu.make_async_copy(block, stack.at[index_ref[k]], sems.at[k])
        for k, block in enumerate(blocks)
    ]
    for copy in copies:
        copy.start()
    for copy in copies:
        copy.wait()


def place(parts):
    count, block = len(parts), parts[0][1]
    shape = jax.ShapeDtypeStruct((count,) + block.shape, block.dtype)
    moved = 2 * count * block.size * block.dtype.itemsize
    return pl.pallas_call(
        place_kernel,
        out_shape=shape,
        in_specs=[pl.BlockSpec(memory_space=pltpu.SMEM)]
        + [pl.BlockSpec(memory_space=pltpu.VMEM)] * count,
        out_specs=pl.BlockSpec(memory_space=pl.ANY),
        scratch_shapes=[pltpu.SemaphoreType.DMA((count,))],
        cost_estimate=pl.CostEstimate(flops=0, bytes_accessed=moved, transcendentals=0),
        compiler_params=pltpu.CompilerParams(vmem_limit_bytes=24 * 2**20),
    )(jnp.stack([jnp.asarray(i, jnp.int32) for i, _ in parts]), *(b for _, b in parts))


def z_gather(block, z, core=None):
    return place([(z, block)] + [((z - hop) % 4, z_send(block, hop, core)) for hop in (1, 2, 3)])


def z_trade(stack, z, core=None):
    return [(z, pick(stack, z))] + [
        ((z - hop) % 4, z_send(pick(stack, (z + hop) % 4), hop, core)) for hop in (1, 2, 3)
    ]


def plane_gather(block, q, core=None):
    return place([(q, block)] + [(q ^ flip, plane_send(block, flip, core)) for flip in (1, 2, 3)])


def plane_trade(stack, q, core=None):
    return place(
        [(q, pick(stack, q))]
        + [(q ^ flip, plane_send(pick(stack, q ^ flip), flip, core)) for flip in (1, 2, 3)]
    )


def plane_sum(partial):
    half = partial.shape[0] // 2
    first, second = partial[:half].astype(low), partial[half:].astype(low)

    def both(mine, flip):
        return mine.astype(wide) + plane_send(mine, flip).astype(wide)

    first, second = both(first, 1).astype(low), both(second, 2).astype(low)
    return jnp.concatenate([both(first, 2), both(second, 1)])


def teams_sum(value):
    flip = TEAM
    while flip < lax.axis_size("replica"):
        sent = value.astype(low)
        value = sent.astype(wide) + plane_send(sent, flip).astype(wide)
        flip *= 2
    return value


def after(value, earlier):
    return lax.optimization_barrier((value, earlier))[0]


def fold(block, width):
    rows, cols = block.shape[-2], block.shape[-1]
    if cols % width == 0:
        return jnp.concatenate(
            [block[..., start : start + width] for start in range(0, cols, width)], axis=-2
        )
    tail = block[..., width:]
    tail = jnp.concatenate([tail[..., : rows // 2, :], tail[..., rows // 2 :, :]], axis=-1)
    return jnp.concatenate([block[..., :width], tail], axis=-2)


def unfold(block, cols):
    width = block.shape[-1]
    if cols % width == 0:
        rows = block.shape[-2] * width // cols
        return jnp.concatenate(
            [block[..., k * rows : (k + 1) * rows, :] for k in range(cols // width)], axis=-1
        )
    rows = block.shape[-2] * width // cols
    tail = block[..., rows:, :]
    tail = jnp.concatenate([tail[..., : width // 2], tail[..., width // 2 :]], axis=-2)
    return jnp.concatenate([block[..., :rows, :], tail], axis=-1)


def tables(segments):
    count = segments.shape[0]
    rows = jnp.arange(count, dtype=jnp.int32)
    before = jnp.sum((segments[None, :] < segments[:, None]).astype(jnp.int32), axis=1)
    allowed = (segments[None, :] == segments[:, None]) & (rows[None, :] <= rows[:, None])
    frequency = rope_base ** (-jnp.arange(HD // 2).astype(wide) * (2.0 / HD))
    angles = (rows - before).astype(wide)[:, None] * frequency[None, :]
    angles = jnp.concatenate([angles, angles], axis=1)
    return allowed, jnp.cos(angles)[:, None, :], jnp.sin(angles)[:, None, :]


def rotate_fwd(values, cos_tab, sin_tab):
    half = HD // 2
    turned = jnp.concatenate([-values[..., half:], values[..., :half]], axis=-1)
    return values * cos_tab + turned * sin_tab


def rotate_back(values, cos_tab, sin_tab):
    half = HD // 2
    shifted = values * sin_tab
    return values * cos_tab + jnp.concatenate([shifted[..., half:], -shifted[..., :half]], axis=-1)


def row_scale(values):
    return lax.rsqrt(jnp.mean(values * values, axis=-1, keepdims=True) + norm_eps)


def norm_back(grad_normed, values, gain):
    factor = row_scale(values)
    gain_grad = jnp.sum(grad_normed * values * factor, axis=0)
    weighted = grad_normed * gain
    inner = jnp.mean(weighted * values, axis=-1, keepdims=True)
    return gain_grad, factor * weighted - values * factor * factor * factor * inner


def attention_fwd(layer_in, tabs, attn_w, gain):
    allowed, cos_tab, sin_tab = tabs
    count = layer_in.shape[0]
    x = layer_in.astype(wide)
    normed = (x * row_scale(x) * gain).astype(low)
    mixed = dot(normed, attn_w[1])
    query_pre = jnp.concatenate([dot(normed, attn_w[0]), mixed[:, :320]], axis=1)
    queries = rotate_fwd(query_pre.reshape(count, QH, HD), cos_tab, sin_tab).astype(low)
    queries = queries.reshape(count, KVH, QH // KVH, HD)
    keys = rotate_fwd(mixed[:, 320:].reshape(count, KVH, HD), cos_tab, sin_tab).astype(low)
    values = dot(normed, attn_w[2][:, :320]).astype(low).reshape(count, KVH, HD)
    scores = jnp.einsum("cgrd,sgd->grcs", queries, keys, preferred_element_type=wide) * HD**-0.5
    scores = jnp.where(allowed[None, None], scores, mask_fill)
    exponent = jnp.exp(scores - jnp.max(scores, axis=-1, keepdims=True))
    probs = exponent / jnp.sum(exponent, axis=-1, keepdims=True)
    attended = jnp.einsum("grcs,sgd->cgrd", probs.astype(low), values, preferred_element_type=wide)
    attended = attended.reshape(count, QH * HD).astype(low)
    branch = jnp.concatenate([dot(attended, attn_w[2][:, 320:]), dot(attended, attn_w[3])], axis=1)
    return x + branch, (normed, queries, keys, values, probs, attended)


def attention_back(layer_in, grad_middle, tabs, attn_w, gain, kept):
    allowed, cos_tab, sin_tab = tabs
    normed, queries, keys, values, probs, attended = kept
    count = layer_in.shape[0]
    branch = grad_middle.astype(low)
    grad_att = dot_t(branch[:, :320], attn_w[2][:, 320:]) + dot_t(branch[:, 320:], attn_w[3])
    grad_att = grad_att.astype(low).reshape(count, KVH, QH // KVH, HD)
    grad_probs = jnp.einsum("cgrd,sgd->grcs", grad_att, values, preferred_element_type=wide)
    centre = jnp.sum(probs * grad_probs, axis=-1, keepdims=True)
    grad_scores = (probs * (grad_probs - centre)).astype(low)
    scale = HD**-0.5
    grad_q = jnp.einsum("grcs,sgd->cgrd", grad_scores, keys, preferred_element_type=wide) * scale
    grad_k = jnp.einsum("grcs,cgrd->sgd", grad_scores, queries, preferred_element_type=wide) * scale
    grad_v = jnp.einsum(
        "grcs,cgrd->sgd", probs.astype(low), grad_att, preferred_element_type=wide
    )
    grad_q = rotate_back(grad_q.reshape(count, QH, HD), cos_tab, sin_tab).astype(low)
    grad_k = rotate_back(grad_k, cos_tab, sin_tab).astype(low)
    pieces = [
        grad_q.reshape(count, QH * HD),
        grad_k.reshape(count, KVH * HD),
        grad_v.astype(low).reshape(count, KVH * HD),
        branch,
    ]
    right = jnp.concatenate(pieces, axis=1)
    grad_normed = (
        dot_t(right[:, :640], attn_w[0])
        + dot_t(right[:, 640:1280], attn_w[1])
        + dot_t(right[:, 1280:1600], attn_w[2][:, :320])
    )
    x = layer_in.astype(wide)
    gain_grad, through = norm_back(grad_normed, x, gain)
    return grad_middle + through, right, gain_grad


def local(
    hidden_in,
    segment_ids,
    norm_attn,
    w_query,
    w_key,
    w_value,
    w_out,
    norm_ffn,
    w_gate,
    w_up,
    w_down,
    out_grad,
):
    core = lax.axis_index("section")
    z = lax.axis_index("shard")
    replica = lax.axis_index("replica")
    q = replica % TEAM
    layers = 2
    group, width = hidden_in.shape[2], hidden_in.shape[3]

    chunk = (w_query.shape[2] * 2 + w_key.shape[2] * 2) // TEAM
    hid = w_gate.shape[2] // TEAM
    down_rows = w_down.shape[1] // TEAM
    attn_all = jnp.concatenate([w_query[0], w_key[0], w_value[0], w_out[0]], axis=1)
    attn_share = lax.dynamic_slice_in_dim(attn_all, q * chunk, chunk, axis=1)
    half, strip = chunk // 2, down_rows // 2
    own_hid = hid // 2

    def ffn_half(which):
        start = q * hid + which * own_hid
        gate, up = (
            lax.dynamic_slice_in_dim(w[0], start, own_hid, axis=1) for w in (w_gate, w_up)
        )
        down = lax.dynamic_slice_in_dim(w_down[0], which * own_hid + q * strip, strip, axis=0)
        return jnp.concatenate([gate, up, fold(down, half)], axis=1)

    ffn_low, ffn_high = ffn_half(0), ffn_half(1)
    ffn_keep = jnp.where(core == 0, ffn_low, ffn_high)
    ffn_got = swap(jnp.where(core == 0, ffn_high, ffn_low))
    ffn_shares = [jnp.where(core == layer, ffn_keep, ffn_got) for layer in range(layers)]

    def give(value, owner):
        return jnp.where(core == owner, value, to_core(value, 1 - owner))

    def both_layers(own):
        other = swap(own)
        return [jnp.where(core == layer, own, other) for layer in range(layers)]

    def whole_sequence(mine):
        blocks = plane_gather(mine, q)
        return lax.all_to_all(blocks, "shard", 0, 0, tiled=False)

    own_segments = lax.dynamic_slice_in_dim(pick(segment_ids[:, 0], core), z * group, group)
    marks = jnp.zeros((16, width), low)
    marks = marks.at[0, :group].set(own_segments.astype(low))
    marks = marks.at[1, : norm_attn.shape[1]].set(norm_attn[0])
    marks = marks.at[2, : norm_ffn.shape[1]].set(norm_ffn[0])
    entry = whole_sequence(jnp.concatenate([pick(hidden_in[:, 0], core), marks]))
    attn_rows = z_gather(attn_share, z, 0).reshape(-1, chunk)
    attn_rows, entry, ffn_shares = lax.optimization_barrier((attn_rows, entry, ffn_shares))
    turn = to_core(attn_rows[:16, :128], 1)
    hidden = entry[:, :group].reshape(-1, width)
    segments = entry[:, group, :group].reshape(-1).astype(jnp.int32)
    tabs = tables(segments)
    own_gains = entry[:, group + 1 : group + 3, : norm_attn.shape[1]]
    gains = both_layers(own_gains.transpose(1, 0, 2).reshape(2, -1))
    gains = [gain.astype(wide) for gain in gains]

    attn_w, ffn_w, down_w = [None] * 2, [None] * 2, [None] * 2
    attn_w[0] = give(plane_gather(attn_rows, q, 0), 0)
    rows = z_gather(after(attn_share, turn), z, 1).reshape(-1, chunk)
    earlier = entry
    for layer in range(layers):
        blocks = lax.all_gather(after(ffn_shares[layer], earlier), "shard")
        own = blocks[:, :, : 2 * own_hid].reshape(-1, 2 * own_hid)
        ffn_w[layer] = (own, swap(own))
        own = unfold(plane_trade(blocks[:, :, 2 * own_hid :], q), width).reshape(-1, width)
        down_w[layer] = (own, swap(own))
        earlier = blocks
    attn_w[1] = give(plane_gather(after(rows, attn_w[0]), q, 1), 1)
    top_grad = whole_sequence(pick(after(out_grad, attn_w[1])[:, 0], core)).reshape(-1, width)

    inputs, kept, outputs = [hidden], [], []
    for layer in range(layers):
        middle, kept_attn = attention_fwd(inputs[layer], tabs, attn_w[layer], gains[layer][0])
        normed = (middle * row_scale(middle) * gains[layer][1]).astype(low)
        gates, ups, acts, partial = [], [], [], 0.0
        for weights, down in zip(ffn_w[layer], down_w[layer]):
            both = dot(normed, weights)
            gate, up = both[:, :own_hid], both[:, own_hid:]
            act = (gate * jax.nn.sigmoid(gate) * up).astype(low)
            partial = partial + dot(act, down)
            gates.append(gate)
            ups.append(up)
            acts.append(act)
        kept.append((kept_attn, middle, normed, gates, ups, acts))
        result = (middle + plane_sum(partial)).astype(low)
        if layer == 0:
            result, top_grad = lax.optimization_barrier((result, top_grad))
        outputs.append(result)
        inputs.append(result)

    def spread(by_layer):
        mine = jnp.where(core == 0, by_layer[0], by_layer[1])
        other = swap(jnp.where(core == 0, by_layer[1], by_layer[0]))
        stack = jnp.where(
            core == 0, jnp.stack([mine, other]), jnp.stack([other, mine])
        ).reshape(2, 4, group, width)
        replicas = lax.axis_size("replica")

        def slice_for(target):
            return lax.dynamic_index_in_dim(stack, target, 1, keepdims=False)

        total = jnp.where(z == q, slice_for(z), 0)
        for hop in (1, 2, 3):
            pairs = [
                ((r % TEAM) * replicas + r, (r % TEAM + hop) % 4 * replicas + r)
                for r in range(replicas)
            ]
            total = total + lax.ppermute(slice_for((z + hop) % 4), ("shard", "replica"), pairs)
        return total[None, :, None]

    def exchange(mine, other):
        return (mine + swap(other.astype(low)).astype(wide)).astype(low)

    def sum_z(stack):
        total = lax.psum_scatter(stack, "shard", scatter_dimension=0, tiled=False)
        return teams_sum(total.astype(wide)).astype(low)

    split = w_query.shape[2] + w_key.shape[2] * 2

    def attn_half(kept_attn, right, which):
        start = q * chunk + which * half
        part = lax.dynamic_slice_in_dim(right, start, half, axis=1)
        column = start + jnp.arange(half)
        return jnp.where(
            column[None, :] < split, dot_l(kept_attn[0], part), dot_l(kept_attn[5], part)
        )

    gain_grads, input_grads = [None] * 2, [None] * 2
    attn_sums, pair_sums = [None] * 2, [None] * 2
    grad = top_grad
    for layer in reversed(range(layers)):
        kept_attn, middle, normed, gates, ups, acts = kept[layer]
        down_part = exchange(*(dot_l(act, grad) for act in acts))
        down_part = plane_trade(down_part.reshape(TEAM, strip, width), q)
        sides, partial = [], 0.0
        for side in (0, 1):
            gate, up = gates[side], ups[side]
            grad_act = dot_t(grad, down_w[layer][side])
            sig = jax.nn.sigmoid(gate)
            grad_gate = (grad_act * up * sig * (1.0 + gate * (1.0 - sig))).astype(low)
            grad_up = (grad_act * gate * sig).astype(low)
            sides.append(jnp.concatenate([grad_gate, grad_up], axis=1))
            partial = partial + dot_t(sides[side], ffn_w[layer][side])
        grad_normed = plane_sum(partial)
        ffn_part = exchange(*(dot_l(normed, part) for part in sides))
        pair = jnp.concatenate(
            [ffn_part.reshape(4, -1, 2 * own_hid), fold(down_part, half)], axis=2
        )
        grad_normed, pair = lax.optimization_barrier((grad_normed, pair))
        if layer == 0:
            grad_normed, pair, layer_out, attn_sums[1] = lax.optimization_barrier(
                (grad_normed, pair, layer_out, attn_sums[1])
            )
        pair_sums[layer] = sum_z(pair)
        gain_ffn, through = norm_back(grad_normed, middle, gains[layer][1])
        grad_middle = grad.astype(wide) + through
        grad_in, right, gain_attn = attention_back(
            inputs[layer], grad_middle, tabs, attn_w[layer], gains[layer][0], kept_attn
        )
        grad = grad_in.astype(low)
        attn_part = exchange(
            attn_half(kept_attn, right, core), attn_half(kept_attn, right, 1 - core)
        )
        attn_part = after(attn_part, pair_sums[layer])
        attn_sums[layer] = sum_z(attn_part.reshape(4, -1, half))
        gain_grads[layer] = jnp.stack([gain_attn, gain_ffn])
        input_grads[layer] = grad
        if layer == 1:
            layer_out = spread(outputs)

    def to_owner(first, second):
        own = jnp.where(core == 0, first, second)
        other = swap(jnp.where(core == 0, second, first))
        return jnp.where(core == 0, own, other), jnp.where(core == 0, other, own)

    whole_1 = plane_gather(jnp.concatenate([pair_sums[1], attn_sums[1]], axis=1), q)
    pair_width = pair_sums[1].shape[1]
    pair_half = to_owner(plane_gather(pair_sums[0], q), whole_1[:, :, :pair_width])
    attn_half_sums = to_owner(plane_gather(attn_sums[0], q), whole_1[:, :, pair_width:])
    input_grad = spread(input_grads)

    gain_all = jnp.stack(gain_grads)
    gain_all = gain_all + swap(gain_all)
    total = gain_all
    for hop in (1, 2, 3):
        total = total + z_send(gain_all, hop)
    flip = TEAM
    while flip < lax.axis_size("replica"):
        total = total + plane_send(total, flip)
        flip *= 2
    total = jnp.where(core == 0, total[0], total[1])
    total = lax.dynamic_index_in_dim(total.reshape(2, 4, -1), z, 1, keepdims=False)

    attn_cols = jnp.concatenate(
        [part[num] for num in range(TEAM) for part in attn_half_sums], axis=1
    ).astype(wide)

    def hidden_cols(start):
        return jnp.concatenate(
            [
                part[num, :, start : start + own_hid]
                for num in range(TEAM)
                for part in pair_half
            ],
            axis=1,
        ).astype(wide)

    gate_cols, up_cols = hidden_cols(0), hidden_cols(own_hid)
    down_sum = jnp.stack(
        [unfold(part[:, :, 2 * own_hid :], width) for part in pair_half]
    ).astype(wide)
    qw, kw = w_query.shape[2], w_key.shape[2]
    return (
        layer_out,
        input_grad,
        total[0][None],
        attn_cols[None, :, :qw],
        attn_cols[None, :, qw : qw + kw],
        attn_cols[None, :, qw + kw : qw + 2 * kw],
        attn_cols[None, :, qw + 2 * kw :],
        total[1][None],
        gate_cols[None],
        up_cols[None],
        down_sum.reshape(1, -1, width),
    )


def solution(mesh):
    placed = (
        P(None, "replica", "shard", None),
        P(None, "replica", None),
        P("section", "shard"),
        P("section", "shard", None),
        P("section", "shard", None),
        P("section", "shard", None),
        P("section", "shard", None),
        P("section", "shard"),
        P("section", "shard", None),
        P("section", "shard", None),
        P("section", "shard", None),
        P(None, "replica", "shard", None),
    )
    return jax.shard_map(
        local,
        mesh=mesh,
        in_specs=placed,
        out_specs=(
            P("section", None, "replica", "shard", None),
            P("section", None, "replica", "shard", None),
            P("section", "shard"),
            P("section", "shard", None),
            P("section", "shard", None),
            P("section", "shard", None),
            P("section", "shard", None),
            P("section", "shard"),
            P("section", "shard", None),
            P("section", "shard", None),
            P("section", "shard", None),
        ),
        check_vma=False,
    )
```

```python
import jax
import jax.numpy as jnp
from jax import lax
from jax.experimental import pallas as pl
from jax.experimental.pallas import tpu as pltpu
from jax.sharding import PartitionSpec as P

QH = 15
KVH = 5
HD = 64
TEAM = 4

rope_base = 100000.0
norm_eps = 1e-05
mask_fill = -1000000000.0

low = jnp.bfloat16
wide = jnp.float32


def dot(a, b):
    return jnp.dot(a, b, preferred_element_type=wide)


def dot_t(a, b):
    return lax.dot_general(a, b, (((1,), (1,)), ((), ())), preferred_element_type=wide)


def dot_l(a, b):
    return lax.dot_general(a, b, (((0,), (0,)), ((), ())), preferred_element_type=wide)


def to_core(value, target):
    return lax.ppermute(value, "section", [(1 - target, target)])


def swap(value):
    return lax.ppermute(value, "section", [(0, 1), (1, 0)])


def z_send(value, hop, core=None):
    count = lax.axis_size("shard")
    cores = range(lax.axis_size("section")) if core is None else (core,)
    pairs = [(c * count + z, c * count + (z + hop) % count) for c in cores for z in range(count)]
    return lax.ppermute(value, ("section", "shard"), pairs)


def plane_send(value, flip, core=None):
    count = lax.axis_size("replica")
    cores = range(lax.axis_size("section")) if core is None else (core,)
    pairs = [(c * count + r, c * count + (r ^ flip)) for c in cores for r in range(count)]
    return lax.ppermute(value, ("section", "replica"), pairs)


def pick(stack, index):
    return lax.dynamic_index_in_dim(stack, index, 0, keepdims=False)


def place_kernel(index_ref, *refs):
    *blocks, stack, sems = refs
    copies = [
        pltpu.make_async_copy(block, stack.at[index_ref[k]], sems.at[k])
        for k, block in enumerate(blocks)
    ]
    for copy in copies:
        copy.start()
    for copy in copies:
        copy.wait()


def place(parts):
    count, block = len(parts), parts[0][1]
    shape = jax.ShapeDtypeStruct((count,) + block.shape, block.dtype)
    moved = 2 * count * block.size * block.dtype.itemsize
    return pl.pallas_call(
        place_kernel,
        out_shape=shape,
        in_specs=[pl.BlockSpec(memory_space=pltpu.SMEM)]
        + [pl.BlockSpec(memory_space=pltpu.VMEM)] * count,
        out_specs=pl.BlockSpec(memory_space=pl.ANY),
        scratch_shapes=[pltpu.SemaphoreType.DMA((count,))],
        cost_estimate=pl.CostEstimate(flops=0, bytes_accessed=moved, transcendentals=0),
        compiler_params=pltpu.CompilerParams(vmem_limit_bytes=24 * 2**20),
    )(jnp.stack([jnp.asarray(i, jnp.int32) for i, _ in parts]), *(b for _, b in parts))


def z_gather(block, z, core=None):
    return place([(z, block)] + [((z - hop) % 4, z_send(block, hop, core)) for hop in (1, 2, 3)])


def z_trade(stack, z, core=None):
    return [(z, pick(stack, z))] + [
        ((z - hop) % 4, z_send(pick(stack, (z + hop) % 4), hop, core)) for hop in (1, 2, 3)
    ]


def plane_gather(block, q, core=None):
    return place([(q, block)] + [(q ^ flip, plane_send(block, flip, core)) for flip in (1, 2, 3)])


def plane_trade(stack, q, core=None):
    return place(
        [(q, pick(stack, q))]
        + [(q ^ flip, plane_send(pick(stack, q ^ flip), flip, core)) for flip in (1, 2, 3)]
    )


def plane_sum(partial):
    half = partial.shape[0] // 2
    first, second = partial[:half].astype(low), partial[half:].astype(low)

    def both(mine, flip):
        return mine.astype(wide) + plane_send(mine, flip).astype(wide)

    first, second = both(first, 1).astype(low), both(second, 2).astype(low)
    return jnp.concatenate([both(first, 2), both(second, 1)])


def teams_sum(value):
    flip = TEAM
    while flip < lax.axis_size("replica"):
        sent = value.astype(low)
        value = sent.astype(wide) + plane_send(sent, flip).astype(wide)
        flip *= 2
    return value


def after(value, earlier):
    return lax.optimization_barrier((value, earlier))[0]


def fold(block, width):
    rows, cols = block.shape[-2], block.shape[-1]
    if cols % width == 0:
        return jnp.concatenate(
            [block[..., start : start + width] for start in range(0, cols, width)], axis=-2
        )
    tail = block[..., width:]
    tail = jnp.concatenate([tail[..., : rows // 2, :], tail[..., rows // 2 :, :]], axis=-1)
    return jnp.concatenate([block[..., :width], tail], axis=-2)


def unfold(block, cols):
    width = block.shape[-1]
    if cols % width == 0:
        rows = block.shape[-2] * width // cols
        return jnp.concatenate(
            [block[..., k * rows : (k + 1) * rows, :] for k in range(cols // width)], axis=-1
        )
    rows = block.shape[-2] * width // cols
    tail = block[..., rows:, :]
    tail = jnp.concatenate([tail[..., : width // 2], tail[..., width // 2 :]], axis=-2)
    return jnp.concatenate([block[..., :rows, :], tail], axis=-1)


def tables(segments):
    count = segments.shape[0]
    rows = jnp.arange(count, dtype=jnp.int32)
    before = jnp.sum((segments[None, :] < segments[:, None]).astype(jnp.int32), axis=1)
    allowed = (segments[None, :] == segments[:, None]) & (rows[None, :] <= rows[:, None])
    frequency = rope_base ** (-jnp.arange(HD // 2).astype(wide) * (2.0 / HD))
    angles = (rows - before).astype(wide)[:, None] * frequency[None, :]
    angles = jnp.concatenate([angles, angles], axis=1)
    return allowed, jnp.cos(angles)[:, None, :], jnp.sin(angles)[:, None, :]


def rotate_fwd(values, cos_tab, sin_tab):
    half = HD // 2
    turned = jnp.concatenate([-values[..., half:], values[..., :half]], axis=-1)
    return values * cos_tab + turned * sin_tab


def rotate_back(values, cos_tab, sin_tab):
    half = HD // 2
    shifted = values * sin_tab
    return values * cos_tab + jnp.concatenate([shifted[..., half:], -shifted[..., :half]], axis=-1)


def row_scale(values):
    return lax.rsqrt(jnp.mean(values * values, axis=-1, keepdims=True) + norm_eps)


def norm_back(grad_normed, values, gain):
    factor = row_scale(values)
    gain_grad = jnp.sum(grad_normed * values * factor, axis=0)
    weighted = grad_normed * gain
    inner = jnp.mean(weighted * values, axis=-1, keepdims=True)
    return gain_grad, factor * weighted - values * factor * factor * factor * inner


def attention_fwd(layer_in, tabs, attn_w, gain):
    allowed, cos_tab, sin_tab = tabs
    count = layer_in.shape[0]
    x = layer_in.astype(wide)
    normed = (x * row_scale(x) * gain).astype(low)
    mixed = dot(normed, attn_w[1])
    query_pre = jnp.concatenate([dot(normed, attn_w[0]), mixed[:, :320]], axis=1)
    queries = rotate_fwd(query_pre.reshape(count, QH, HD), cos_tab, sin_tab).astype(low)
    queries = queries.reshape(count, KVH, QH // KVH, HD)
    keys = rotate_fwd(mixed[:, 320:].reshape(count, KVH, HD), cos_tab, sin_tab).astype(low)
    values = dot(normed, attn_w[2][:, :320]).astype(low).reshape(count, KVH, HD)
    scores = jnp.einsum("cgrd,sgd->grcs", queries, keys, preferred_element_type=wide) * HD**-0.5
    scores = jnp.where(allowed[None, None], scores, mask_fill)
    exponent = jnp.exp(scores - jnp.max(scores, axis=-1, keepdims=True))
    probs = exponent / jnp.sum(exponent, axis=-1, keepdims=True)
    attended = jnp.einsum("grcs,sgd->cgrd", probs.astype(low), values, preferred_element_type=wide)
    attended = attended.reshape(count, QH * HD).astype(low)
    branch = jnp.concatenate([dot(attended, attn_w[2][:, 320:]), dot(attended, attn_w[3])], axis=1)
    return x + branch, (normed, queries, keys, values, probs, attended)


def attention_back(layer_in, grad_middle, tabs, attn_w, gain, kept):
    allowed, cos_tab, sin_tab = tabs
    normed, queries, keys, values, probs, attended = kept
    count = layer_in.shape[0]
    branch = grad_middle.astype(low)
    grad_att = dot_t(branch[:, :320], attn_w[2][:, 320:]) + dot_t(branch[:, 320:], attn_w[3])
    grad_att = grad_att.astype(low).reshape(count, KVH, QH // KVH, HD)
    grad_probs = jnp.einsum("cgrd,sgd->grcs", grad_att, values, preferred_element_type=wide)
    centre = jnp.sum(probs * grad_probs, axis=-1, keepdims=True)
    grad_scores = (probs * (grad_probs - centre)).astype(low)
    scale = HD**-0.5
    grad_q = jnp.einsum("grcs,sgd->cgrd", grad_scores, keys, preferred_element_type=wide) * scale
    grad_k = jnp.einsum("grcs,cgrd->sgd", grad_scores, queries, preferred_element_type=wide) * scale
    grad_v = jnp.einsum(
        "grcs,cgrd->sgd", probs.astype(low), grad_att, preferred_element_type=wide
    )
    grad_q = rotate_back(grad_q.reshape(count, QH, HD), cos_tab, sin_tab).astype(low)
    grad_k = rotate_back(grad_k, cos_tab, sin_tab).astype(low)
    pieces = [
        grad_q.reshape(count, QH * HD),
        grad_k.reshape(count, KVH * HD),
        grad_v.astype(low).reshape(count, KVH * HD),
        branch,
    ]
    right = jnp.concatenate(pieces, axis=1)
    grad_normed = (
        dot_t(right[:, :640], attn_w[0])
        + dot_t(right[:, 640:1280], attn_w[1])
        + dot_t(right[:, 1280:1600], attn_w[2][:, :320])
    )
    x = layer_in.astype(wide)
    gain_grad, through = norm_back(grad_normed, x, gain)
    return grad_middle + through, right, gain_grad


def local(
    hidden_in,
    segment_ids,
    norm_attn,
    w_query,
    w_key,
    w_value,
    w_out,
    norm_ffn,
    w_gate,
    w_up,
    w_down,
    out_grad,
):
    core = lax.axis_index("section")
    z = lax.axis_index("shard")
    replica = lax.axis_index("replica")
    q = replica % TEAM
    layers = 2
    group, width = hidden_in.shape[2], hidden_in.shape[3]

    chunk = (w_query.shape[2] * 2 + w_key.shape[2] * 2) // TEAM
    hid = w_gate.shape[2] // TEAM
    down_rows = w_down.shape[1] // TEAM
    attn_all = jnp.concatenate([w_query[0], w_key[0], w_value[0], w_out[0]], axis=1)
    attn_share = lax.dynamic_slice_in_dim(attn_all, q * chunk, chunk, axis=1)
    half, strip = chunk // 2, down_rows // 2
    own_hid = hid // 2

    def ffn_half(which):
        start = q * hid + which * own_hid
        gate, up = (
            lax.dynamic_slice_in_dim(w[0], start, own_hid, axis=1) for w in (w_gate, w_up)
        )
        down = lax.dynamic_slice_in_dim(w_down[0], which * own_hid + q * strip, strip, axis=0)
        return jnp.concatenate([gate, up, fold(down, half)], axis=1)

    ffn_low, ffn_high = ffn_half(0), ffn_half(1)
    ffn_keep = jnp.where(core == 0, ffn_low, ffn_high)
    ffn_got = swap(jnp.where(core == 0, ffn_high, ffn_low))
    ffn_shares = [jnp.where(core == layer, ffn_keep, ffn_got) for layer in range(layers)]

    def give(value, owner):
        return jnp.where(core == owner, value, to_core(value, 1 - owner))

    def both_layers(own):
        other = swap(own)
        return [jnp.where(core == layer, own, other) for layer in range(layers)]

    def whole_sequence(mine):
        blocks = plane_gather(mine, q)
        return lax.all_to_all(blocks, "shard", 0, 0, tiled=False)

    own_segments = lax.dynamic_slice_in_dim(pick(segment_ids[:, 0], core), z * group, group)
    marks = jnp.zeros((16, width), low)
    marks = marks.at[0, :group].set(own_segments.astype(low))
    marks = marks.at[1, : norm_attn.shape[1]].set(norm_attn[0])
    marks = marks.at[2, : norm_ffn.shape[1]].set(norm_ffn[0])
    entry = whole_sequence(
        jnp.concatenate([pick(hidden_in[:, 0], core), pick(out_grad[:, 0], core), marks])
    )
    attn_rows = z_gather(attn_share, z, 0).reshape(-1, chunk)
    attn_rows, entry = lax.optimization_barrier((attn_rows, entry))
    turn = to_core(attn_rows[:16, :128], 1)
    hidden = entry[:, :group].reshape(-1, width)
    top_grad = entry[:, group : 2 * group].reshape(-1, width)
    entry_marks = entry[:, 2 * group :]
    segments = entry_marks[:, 0, :group].reshape(-1).astype(jnp.int32)
    tabs = tables(segments)
    own_gains = entry_marks[:, 1:3, : norm_attn.shape[1]]
    gains = both_layers(own_gains.transpose(1, 0, 2).reshape(2, -1))
    gains = [gain.astype(wide) for gain in gains]

    attn_w, ffn_w, down_w = [None] * 2, [None] * 2, [None] * 2
    rows = z_gather(after(attn_share, turn), z, 1).reshape(-1, chunk)
    blocks = [lax.all_gather(after(ffn_shares[0], entry), "shard"), None]
    attn_stack, blocks[0] = lax.optimization_barrier((plane_gather(attn_rows, q, 0), blocks[0]))
    blocks[1] = lax.all_gather(after(ffn_shares[1], blocks[0]), "shard")
    attn_w[0] = give(attn_stack, 0)

    def unpack(stack):
        own = stack[:, :, : 2 * own_hid].reshape(-1, 2 * own_hid)
        down = unfold(plane_trade(stack[:, :, 2 * own_hid :], q), width).reshape(-1, width)
        return (own, swap(own)), (down, swap(down))

    ffn_w[0], down_w[0] = unpack(blocks[0])
    attn_w[1] = give(plane_gather(after(rows, attn_w[0]), q, 1), 1)

    inputs, kept, outputs = [hidden], [], []
    for layer in range(layers):
        middle, kept_attn = attention_fwd(inputs[layer], tabs, attn_w[layer], gains[layer][0])
        if layer == 0:
            middle, second = lax.optimization_barrier((middle, blocks[1]))
            ffn_w[1], down_w[1] = unpack(second)
        normed = (middle * row_scale(middle) * gains[layer][1]).astype(low)
        gates, ups, acts, partial = [], [], [], 0.0
        for weights, down in zip(ffn_w[layer], down_w[layer]):
            both = dot(normed, weights)
            gate, up = both[:, :own_hid], both[:, own_hid:]
            act = (gate * jax.nn.sigmoid(gate) * up).astype(low)
            partial = partial + dot(act, down)
            gates.append(gate)
            ups.append(up)
            acts.append(act)
        kept.append((kept_attn, middle, normed, gates, ups, acts))
        if layer < layers - 1:
            result = (middle + plane_sum(partial)).astype(low)
            outputs.append(result)
            inputs.append(result)

    def spread(by_layer):
        mine = jnp.where(core == 0, by_layer[0], by_layer[1])
        other = swap(jnp.where(core == 0, by_layer[1], by_layer[0]))
        stack = jnp.where(
            core == 0, jnp.stack([mine, other]), jnp.stack([other, mine])
        ).reshape(2, 4, group, width)
        replicas = lax.axis_size("replica")

        def slice_for(target):
            return lax.dynamic_index_in_dim(stack, target, 1, keepdims=False)

        total = jnp.where(z == q, slice_for(z), 0)
        for hop in (1, 2, 3):
            pairs = [
                ((r % TEAM) * replicas + r, (r % TEAM + hop) % 4 * replicas + r)
                for r in range(replicas)
            ]
            total = total + lax.ppermute(slice_for((z + hop) % 4), ("shard", "replica"), pairs)
        return total[None, :, None]

    def exchange(mine, other):
        return (mine + swap(other.astype(low)).astype(wide)).astype(low)

    def sum_z(stack):
        total = lax.psum_scatter(stack, "shard", scatter_dimension=0, tiled=False)
        return teams_sum(total.astype(wide)).astype(low)

    split = w_query.shape[2] + w_key.shape[2] * 2

    def gather_halves(own, owner):
        other = to_core(own, owner)
        return jnp.concatenate([own, other] if owner == 0 else [other, own], axis=1)

    def attn_half(kept_attn, right, which):
        start = q * chunk + which * half
        part = lax.dynamic_slice_in_dim(right, start, half, axis=1)
        column = start + jnp.arange(half)
        return jnp.where(
            column[None, :] < split, dot_l(kept_attn[0], part), dot_l(kept_attn[5], part)
        )

    gain_grads, input_grads = [None] * 2, [None] * 2
    attn_sums, pair_sums = [None] * 2, [None] * 2
    grad = top_grad
    for layer in reversed(range(layers)):
        kept_attn, middle, normed, gates, ups, acts = kept[layer]
        down_part = exchange(*(dot_l(act, grad) for act in acts))
        down_part = plane_trade(down_part.reshape(TEAM, strip, width), q)
        sides, grad_partial = [], 0.0
        for side in (0, 1):
            gate, up = gates[side], ups[side]
            grad_act = dot_t(grad, down_w[layer][side])
            sig = jax.nn.sigmoid(gate)
            grad_gate = (grad_act * up * sig * (1.0 + gate * (1.0 - sig))).astype(low)
            grad_up = (grad_act * gate * sig).astype(low)
            sides.append(jnp.concatenate([grad_gate, grad_up], axis=1))
            grad_partial = grad_partial + dot_t(sides[side], ffn_w[layer][side])
        grad_normed = plane_sum(grad_partial)
        ffn_part = exchange(*(dot_l(normed, part) for part in sides))
        pair = jnp.concatenate(
            [ffn_part.reshape(4, -1, 2 * own_hid), fold(down_part, half)], axis=2
        )
        grad_normed, pair = lax.optimization_barrier((grad_normed, pair))
        if layer == 0:
            grad_normed, pair, layer_out, attn_sums[1] = lax.optimization_barrier(
                (grad_normed, pair, layer_out, attn_sums[1])
            )
        pair_sums[layer] = sum_z(pair)
        gain_ffn, through = norm_back(grad_normed, middle, gains[layer][1])
        grad_middle = grad.astype(wide) + through
        grad_in, right, gain_attn = attention_back(
            inputs[layer], grad_middle, tabs, attn_w[layer], gains[layer][0], kept_attn
        )
        grad = grad_in.astype(low)
        gain_grads[layer] = jnp.stack([gain_attn, gain_ffn])
        input_grads[layer] = grad
        attn_part = exchange(
            attn_half(kept_attn, right, core), attn_half(kept_attn, right, 1 - core)
        ).reshape(4, -1, half)
        if layer == 1:
            result = (middle + plane_sum(after(partial, grad_normed))).astype(low)
            grad, result = lax.optimization_barrier((grad, result))
            outputs.append(result)
            layer_out = spread(outputs)
        else:
            gain_part = exchange(
                jnp.where(core == 0, gain_grads[0], gain_grads[1]),
                jnp.where(core == 0, gain_grads[1], gain_grads[0]),
            )
            gain_part = gain_part.reshape(2, 4, -1).transpose(1, 0, 2)
            gain_width = gain_part.shape[2]
            gain_part = jnp.pad(gain_part, ((0, 0), (0, 14), (0, half - gain_width)))
            attn_part = jnp.concatenate([attn_part, gain_part], axis=1)
            input_grad = spread(input_grads)
        if layer == 0:
            pair_sums[0], input_grad, whole_1 = lax.optimization_barrier(
                (pair_sums[0], input_grad, whole_1)
            )
        attn_part = after(attn_part, pair_sums[layer])
        attn_sums[layer] = sum_z(attn_part)
        if layer == 1:
            pair_width = pair_sums[1].shape[1]
            whole_1 = plane_gather(
                gather_halves(jnp.concatenate([pair_sums[1], attn_sums[1]], axis=1), 1), q, 1
            )

    gain_rows = attn_sums[0].shape[0] - 16
    total = attn_sums[0][gain_rows : gain_rows + 2, :gain_width].astype(wide)
    pair_0 = plane_gather(gather_halves(pair_sums[0], 0), q, 0)
    attn_0 = plane_gather(gather_halves(attn_sums[0][:gain_rows], 0), q, 0)
    whole_width = pair_width + half
    pair_half = [
        jnp.where(
            core == 0,
            pair_0[:, :, c * pair_width :][:, :, :pair_width],
            whole_1[:, :, c * whole_width :][:, :, :pair_width],
        )
        for c in (0, 1)
    ]
    attn_half_sums = [
        jnp.where(
            core == 0,
            attn_0[:, :, c * half :][:, :, :half],
            whole_1[:, :, c * whole_width + pair_width :][:, :, :half],
        )
        for c in (0, 1)
    ]

    attn_cols = jnp.concatenate(
        [part[num] for num in range(TEAM) for part in attn_half_sums], axis=1
    ).astype(wide)

    def hidden_cols(start):
        return jnp.concatenate(
            [
                part[num, :, start : start + own_hid]
                for num in range(TEAM)
                for part in pair_half
            ],
            axis=1,
        ).astype(wide)

    gate_cols, up_cols = hidden_cols(0), hidden_cols(own_hid)
    down_sum = jnp.stack(
        [unfold(part[:, :, 2 * own_hid :], width) for part in pair_half]
    ).astype(wide)
    qw, kw = w_query.shape[2], w_key.shape[2]
    return (
        layer_out,
        input_grad,
        total[0][None],
        attn_cols[None, :, :qw],
        attn_cols[None, :, qw : qw + kw],
        attn_cols[None, :, qw + kw : qw + 2 * kw],
        attn_cols[None, :, qw + 2 * kw :],
        total[1][None],
        gate_cols[None],
        up_cols[None],
        down_sum.reshape(1, -1, width),
    )


def solution(mesh):
    placed = (
        P(None, "replica", "shard", None),
        P(None, "replica", None),
        P("section", "shard"),
        P("section", "shard", None),
        P("section", "shard", None),
        P("section", "shard", None),
        P("section", "shard", None),
        P("section", "shard"),
        P("section", "shard", None),
        P("section", "shard", None),
        P("section", "shard", None),
        P(None, "replica", "shard", None),
    )
    return jax.shard_map(
        local,
        mesh=mesh,
        in_specs=placed,
        out_specs=(
            P("section", None, "replica", "shard", None),
            P("section", None, "replica", "shard", None),
            P("section", "shard"),
            P("section", "shard", None),
            P("section", "shard", None),
            P("section", "shard", None),
            P("section", "shard", None),
            P("section", "shard"),
            P("section", "shard", None),
            P("section", "shard", None),
            P("section", "shard", None),
        ),
        check_vma=False,
    )
```

```python
import jax
import jax.numpy as jnp
from jax import lax
from jax.experimental import pallas as pl
from jax.experimental.pallas import tpu as pltpu
from jax.sharding import PartitionSpec as P

QH = 15
KVH = 5
HD = 64
TEAM = 4

rope_base = 100000.0
norm_eps = 1e-05
mask_fill = -1000000000.0

low = jnp.bfloat16
wide = jnp.float32


def dot(a, b):
    return jnp.dot(a, b, preferred_element_type=wide)


def dot_t(a, b):
    return lax.dot_general(a, b, (((1,), (1,)), ((), ())), preferred_element_type=wide)


def dot_l(a, b):
    return lax.dot_general(a, b, (((0,), (0,)), ((), ())), preferred_element_type=wide)


def to_core(value, target):
    return lax.ppermute(value, "section", [(1 - target, target)])


def swap(value):
    return lax.ppermute(value, "section", [(0, 1), (1, 0)])


def z_send(value, hop, core=None):
    count = lax.axis_size("shard")
    cores = range(lax.axis_size("section")) if core is None else (core,)
    pairs = [(c * count + z, c * count + (z + hop) % count) for c in cores for z in range(count)]
    return lax.ppermute(value, ("section", "shard"), pairs)


def plane_send(value, flip, core=None):
    count = lax.axis_size("replica")
    cores = range(lax.axis_size("section")) if core is None else (core,)
    pairs = [(c * count + r, c * count + (r ^ flip)) for c in cores for r in range(count)]
    return lax.ppermute(value, ("section", "replica"), pairs)


def turn_over(value):
    count = lax.axis_size("replica")
    pairs = [
        (b * count + r, (r % TEAM) * count + r - r % TEAM + b)
        for b in range(TEAM)
        for r in range(count)
    ]
    return lax.ppermute(value, ("shard", "replica"), pairs)


def pick(stack, index):
    return lax.dynamic_index_in_dim(stack, index, 0, keepdims=False)


def place_kernel(index_ref, *refs):
    *blocks, stack, sems = refs
    copies = [
        pltpu.make_async_copy(block, stack.at[index_ref[k]], sems.at[k])
        for k, block in enumerate(blocks)
    ]
    for copy in copies:
        copy.start()
    for copy in copies:
        copy.wait()


def place(parts):
    count, block = len(parts), parts[0][1]
    shape = jax.ShapeDtypeStruct((count,) + block.shape, block.dtype)
    moved = 2 * count * block.size * block.dtype.itemsize
    return pl.pallas_call(
        place_kernel,
        out_shape=shape,
        in_specs=[pl.BlockSpec(memory_space=pltpu.SMEM)]
        + [pl.BlockSpec(memory_space=pltpu.VMEM)] * count,
        out_specs=pl.BlockSpec(memory_space=pl.ANY),
        scratch_shapes=[pltpu.SemaphoreType.DMA((count,))],
        cost_estimate=pl.CostEstimate(flops=0, bytes_accessed=moved, transcendentals=0),
        compiler_params=pltpu.CompilerParams(vmem_limit_bytes=24 * 2**20),
    )(jnp.stack([jnp.asarray(i, jnp.int32) for i, _ in parts]), *(b for _, b in parts))


def z_gather(block, z, core=None):
    return place([(z, block)] + [((z - hop) % 4, z_send(block, hop, core)) for hop in (1, 2, 3)])


def z_trade(stack, z, core=None):
    return [(z, pick(stack, z))] + [
        ((z - hop) % 4, z_send(pick(stack, (z + hop) % 4), hop, core)) for hop in (1, 2, 3)
    ]


def plane_gather(block, q, core=None):
    return place([(q, block)] + [(q ^ flip, plane_send(block, flip, core)) for flip in (1, 2, 3)])


def plane_trade(stack, q, core=None):
    return place(
        [(q, pick(stack, q))]
        + [(q ^ flip, plane_send(pick(stack, q ^ flip), flip, core)) for flip in (1, 2, 3)]
    )


def plane_sum(partial):
    half = partial.shape[0] // 2
    first, second = partial[:half].astype(low), partial[half:].astype(low)

    def both(mine, flip):
        return mine.astype(wide) + plane_send(mine, flip).astype(wide)

    first, second = both(first, 1).astype(low), both(second, 2).astype(low)
    return jnp.concatenate([both(first, 2), both(second, 1)])


def teams_sum(value):
    flip = TEAM
    while flip < lax.axis_size("replica"):
        sent = value.astype(low)
        value = sent.astype(wide) + plane_send(sent, flip).astype(wide)
        flip *= 2
    return value


def after(value, earlier):
    return lax.optimization_barrier((value, earlier))[0]


def fold(block, width):
    rows, cols = block.shape[-2], block.shape[-1]
    if cols % width == 0:
        return jnp.concatenate(
            [block[..., start : start + width] for start in range(0, cols, width)], axis=-2
        )
    tail = block[..., width:]
    tail = jnp.concatenate([tail[..., : rows // 2, :], tail[..., rows // 2 :, :]], axis=-1)
    return jnp.concatenate([block[..., :width], tail], axis=-2)


def unfold(block, cols):
    width = block.shape[-1]
    if cols % width == 0:
        rows = block.shape[-2] * width // cols
        return jnp.concatenate(
            [block[..., k * rows : (k + 1) * rows, :] for k in range(cols // width)], axis=-1
        )
    rows = block.shape[-2] * width // cols
    tail = block[..., rows:, :]
    tail = jnp.concatenate([tail[..., : width // 2], tail[..., width // 2 :]], axis=-2)
    return jnp.concatenate([block[..., :rows, :], tail], axis=-1)


def tables(segments):
    count = segments.shape[0]
    rows = jnp.arange(count, dtype=jnp.int32)
    before = jnp.sum((segments[None, :] < segments[:, None]).astype(jnp.int32), axis=1)
    allowed = (segments[None, :] == segments[:, None]) & (rows[None, :] <= rows[:, None])
    frequency = rope_base ** (-jnp.arange(HD // 2).astype(wide) * (2.0 / HD))
    angles = (rows - before).astype(wide)[:, None] * frequency[None, :]
    angles = jnp.concatenate([angles, angles], axis=1)
    return allowed, jnp.cos(angles)[:, None, :], jnp.sin(angles)[:, None, :]


def rotate_fwd(values, cos_tab, sin_tab):
    half = HD // 2
    turned = jnp.concatenate([-values[..., half:], values[..., :half]], axis=-1)
    return values * cos_tab + turned * sin_tab


def rotate_back(values, cos_tab, sin_tab):
    half = HD // 2
    shifted = values * sin_tab
    return values * cos_tab + jnp.concatenate([shifted[..., half:], -shifted[..., :half]], axis=-1)


def row_scale(values):
    return lax.rsqrt(jnp.mean(values * values, axis=-1, keepdims=True) + norm_eps)


def norm_back(grad_normed, values, gain):
    factor = row_scale(values)
    gain_grad = jnp.sum(grad_normed * values * factor, axis=0)
    weighted = grad_normed * gain
    inner = jnp.mean(weighted * values, axis=-1, keepdims=True)
    return gain_grad, factor * weighted - values * factor * factor * factor * inner


def attention_fwd(layer_in, tabs, attn_w, gain, blocks):
    allowed, cos_tab, sin_tab = tabs
    count = layer_in.shape[0]
    x = layer_in.astype(wide)
    normed = (x * row_scale(x) * gain).astype(low)
    mixed = dot(normed, attn_w[1])
    query_pre = jnp.concatenate([dot(normed, attn_w[0]), mixed[:, :320]], axis=1)
    queries = rotate_fwd(query_pre.reshape(count, QH, HD), cos_tab, sin_tab).astype(low)
    queries = queries.reshape(count, KVH, QH // KVH, HD)
    keys = rotate_fwd(mixed[:, 320:].reshape(count, KVH, HD), cos_tab, sin_tab).astype(low)
    values = dot(normed, attn_w[2][:, :320]).astype(low).reshape(count, KVH, HD)
    values, blocks = lax.optimization_barrier((values, blocks))
    scores = jnp.einsum("cgrd,sgd->grcs", queries, keys, preferred_element_type=wide) * HD**-0.5
    scores = jnp.where(allowed[None, None], scores, mask_fill)
    exponent = jnp.exp(scores - jnp.max(scores, axis=-1, keepdims=True))
    probs = exponent / jnp.sum(exponent, axis=-1, keepdims=True)
    attended = jnp.einsum("grcs,sgd->cgrd", probs.astype(low), values, preferred_element_type=wide)
    attended = attended.reshape(count, QH * HD).astype(low)
    branch = jnp.concatenate([dot(attended, attn_w[2][:, 320:]), dot(attended, attn_w[3])], axis=1)
    return x + branch, (normed, queries, keys, values, probs, attended), blocks


def attention_back(layer_in, grad_middle, tabs, attn_w, gain, kept):
    allowed, cos_tab, sin_tab = tabs
    normed, queries, keys, values, probs, attended = kept
    count = layer_in.shape[0]
    branch = grad_middle.astype(low)
    grad_att = dot_t(branch[:, :320], attn_w[2][:, 320:]) + dot_t(branch[:, 320:], attn_w[3])
    grad_att = grad_att.astype(low).reshape(count, KVH, QH // KVH, HD)
    grad_probs = jnp.einsum("cgrd,sgd->grcs", grad_att, values, preferred_element_type=wide)
    centre = jnp.sum(probs * grad_probs, axis=-1, keepdims=True)
    grad_scores = (probs * (grad_probs - centre)).astype(low)
    scale = HD**-0.5
    grad_q = jnp.einsum("grcs,sgd->cgrd", grad_scores, keys, preferred_element_type=wide) * scale
    grad_k = jnp.einsum("grcs,cgrd->sgd", grad_scores, queries, preferred_element_type=wide) * scale
    grad_v = jnp.einsum(
        "grcs,cgrd->sgd", probs.astype(low), grad_att, preferred_element_type=wide
    )
    grad_q = rotate_back(grad_q.reshape(count, QH, HD), cos_tab, sin_tab).astype(low)
    grad_k = rotate_back(grad_k, cos_tab, sin_tab).astype(low)
    pieces = [
        grad_q.reshape(count, QH * HD),
        grad_k.reshape(count, KVH * HD),
        grad_v.astype(low).reshape(count, KVH * HD),
        branch,
    ]
    right = jnp.concatenate(pieces, axis=1)
    grad_normed = (
        dot_t(right[:, :640], attn_w[0])
        + dot_t(right[:, 640:1280], attn_w[1])
        + dot_t(right[:, 1280:1600], attn_w[2][:, :320])
    )
    x = layer_in.astype(wide)
    gain_grad, through = norm_back(grad_normed, x, gain)
    return grad_middle + through, right, gain_grad


def local(
    hidden_in,
    segment_ids,
    norm_attn,
    w_query,
    w_key,
    w_value,
    w_out,
    norm_ffn,
    w_gate,
    w_up,
    w_down,
    out_grad,
):
    core = lax.axis_index("section")
    z = lax.axis_index("shard")
    replica = lax.axis_index("replica")
    q = replica % TEAM
    layers = 2
    group, width = hidden_in.shape[2], hidden_in.shape[3]

    chunk = (w_query.shape[2] * 2 + w_key.shape[2] * 2) // TEAM
    hid = w_gate.shape[2] // TEAM
    down_rows = w_down.shape[1] // TEAM
    attn_all = jnp.concatenate([w_query[0], w_key[0], w_value[0], w_out[0]], axis=1)
    attn_share = lax.dynamic_slice_in_dim(attn_all, q * chunk, chunk, axis=1)
    half, strip = chunk // 2, down_rows // 2
    own_hid = hid // 2

    def ffn_half(which):
        start = q * hid + which * own_hid
        gate, up = (
            lax.dynamic_slice_in_dim(w[0], start, own_hid, axis=1) for w in (w_gate, w_up)
        )
        down = lax.dynamic_slice_in_dim(w_down[0], which * own_hid + q * strip, strip, axis=0)
        return jnp.concatenate([gate, up, fold(down, half)], axis=1)

    ffn_low, ffn_high = ffn_half(0), ffn_half(1)
    ffn_keep = jnp.where(core == 0, ffn_low, ffn_high)
    ffn_got = swap(jnp.where(core == 0, ffn_high, ffn_low))
    ffn_shares = [jnp.where(core == layer, ffn_keep, ffn_got) for layer in range(layers)]

    def give(value, owner):
        return jnp.where(core == owner, value, to_core(value, 1 - owner))

    def both_layers(own):
        other = swap(own)
        return [jnp.where(core == layer, own, other) for layer in range(layers)]

    own_segments = lax.dynamic_slice_in_dim(pick(segment_ids[:, 0], core), z * group, group)
    marks = jnp.zeros((16, width), low)
    marks = marks.at[0, :group].set(own_segments.astype(low))
    marks = marks.at[1, : norm_attn.shape[1]].set(norm_attn[0])
    marks = marks.at[2, : norm_ffn.shape[1]].set(norm_ffn[0])
    entry = jnp.concatenate([pick(hidden_in[:, 0], core), pick(out_grad[:, 0], core), marks])
    attn_rows = z_gather(attn_share, z, 0).reshape(-1, chunk)
    attn_rows, entry, ffn_shares = lax.optimization_barrier(
        (attn_rows, turn_over(entry), ffn_shares)
    )
    entry = plane_gather(entry, q)
    turn = to_core(attn_rows[:16, :128], 1)
    hidden = entry[:, :group].reshape(-1, width)
    top_grad = entry[:, group : 2 * group].reshape(-1, width)
    entry_marks = entry[:, 2 * group :]
    segments = entry_marks[:, 0, :group].reshape(-1).astype(jnp.int32)
    tabs = tables(segments)
    own_gains = entry_marks[:, 1:3, : norm_attn.shape[1]]
    gains = both_layers(own_gains.transpose(1, 0, 2).reshape(2, -1))
    gains = [gain.astype(wide) for gain in gains]

    attn_w, ffn_w, down_w = [None] * 2, [None] * 2, [None] * 2
    rows = z_gather(after(attn_share, turn), z, 1).reshape(-1, chunk)
    blocks = [lax.all_gather(ffn_shares[0], "shard"), None]
    attn_stack, gains, blocks[0], ffn_shares[1] = lax.optimization_barrier(
        (plane_gather(attn_rows, q, 0), gains, blocks[0], ffn_shares[1])
    )
    blocks[1] = lax.all_gather(ffn_shares[1], "shard")
    attn_w[0] = give(attn_stack, 0)

    def unpack(stack):
        own = stack[:, :, : 2 * own_hid].reshape(-1, 2 * own_hid)
        down = unfold(plane_trade(stack[:, :, 2 * own_hid :], q), width).reshape(-1, width)
        return (own, swap(own)), (down, swap(down))

    attn_w[1] = give(plane_gather(after(rows, attn_w[0]), q, 1), 1)

    inputs, kept, outputs = [hidden], [], []
    for layer in range(layers):
        middle, kept_attn, ready = attention_fwd(
            inputs[layer], tabs, attn_w[layer], gains[layer][0], blocks[0] if layer == 0 else ()
        )
        if layer == 0:
            ffn_w[0], down_w[0] = unpack(ready)
        normed = (middle * row_scale(middle) * gains[layer][1]).astype(low)
        gates, ups, acts, partial = [], [], [], 0.0
        for weights, down in zip(ffn_w[layer], down_w[layer]):
            both = dot(normed, weights)
            gate, up = both[:, :own_hid], both[:, own_hid:]
            act = (gate * jax.nn.sigmoid(gate) * up).astype(low)
            partial = partial + dot(act, down)
            gates.append(gate)
            ups.append(up)
            acts.append(act)
        kept.append((kept_attn, middle, normed, gates, ups, acts))
        if layer < layers - 1:
            result = (middle + plane_sum(partial)).astype(low)
            result, second = lax.optimization_barrier((result, blocks[1]))
            ffn_w[1], down_w[1] = unpack(second)
            outputs.append(result)
            inputs.append(result)

    def spread(by_layer):
        mine = jnp.where(core == 0, by_layer[0], by_layer[1])
        other = swap(jnp.where(core == 0, by_layer[1], by_layer[0]))
        stack = jnp.where(
            core == 0, jnp.stack([mine, other]), jnp.stack([other, mine])
        ).reshape(2, 4, group, width)
        return turn_over(lax.dynamic_index_in_dim(stack, q, 1, keepdims=False))[None, :, None]

    def exchange(mine, other):
        return (mine + swap(other.astype(low)).astype(wide)).astype(low)

    def sum_z(stack):
        total = lax.psum_scatter(stack, "shard", scatter_dimension=0, tiled=False)
        return teams_sum(total.astype(wide)).astype(low)

    split = w_query.shape[2] + w_key.shape[2] * 2

    def attn_half(kept_attn, right, which):
        start = q * chunk + which * half
        part = lax.dynamic_slice_in_dim(right, start, half, axis=1)
        column = start + jnp.arange(half)
        return jnp.where(
            column[None, :] < split, dot_l(kept_attn[0], part), dot_l(kept_attn[5], part)
        )

    gain_grads, input_grads = [None] * 2, [None] * 2
    attn_parts, pair_sums = [None] * 2, [None] * 2
    grad = top_grad
    for layer in reversed(range(layers)):
        kept_attn, middle, normed, gates, ups, acts = kept[layer]
        down_part = exchange(*(dot_l(act, grad) for act in acts))
        down_part = plane_trade(down_part.reshape(TEAM, strip, width), q)
        sides, grad_partial = [], 0.0
        for side in (0, 1):
            gate, up = gates[side], ups[side]
            grad_act = dot_t(grad, down_w[layer][side])
            sig = jax.nn.sigmoid(gate)
            grad_gate = (grad_act * up * sig * (1.0 + gate * (1.0 - sig))).astype(low)
            grad_up = (grad_act * gate * sig).astype(low)
            sides.append(jnp.concatenate([grad_gate, grad_up], axis=1))
            grad_partial = grad_partial + dot_t(sides[side], ffn_w[layer][side])
        grad_normed = plane_sum(grad_partial)
        ffn_part = exchange(*(dot_l(normed, part) for part in sides))
        pair = jnp.concatenate(
            [ffn_part.reshape(4, -1, 2 * own_hid), fold(down_part, half)], axis=2
        )
        grad_normed, pair = lax.optimization_barrier((grad_normed, pair))
        if layer == 0:
            grad_normed, pair, pair_sums[1] = lax.optimization_barrier(
                (grad_normed, pair, pair_sums[1])
            )
        pair_sums[layer] = sum_z(pair)
        gain_ffn, through = norm_back(grad_normed, middle, gains[layer][1])
        grad_middle = grad.astype(wide) + through
        grad_in, right, gain_attn = attention_back(
            inputs[layer], grad_middle, tabs, attn_w[layer], gains[layer][0], kept_attn
        )
        grad = grad_in.astype(low)
        gain_grads[layer] = jnp.stack([gain_attn, gain_ffn])
        input_grads[layer] = grad
        attn_part = exchange(
            attn_half(kept_attn, right, core), attn_half(kept_attn, right, 1 - core)
        ).reshape(4, -1, half)
        if layer == 1:
            result = (middle + plane_sum(after(partial, grad_normed))).astype(low)
            grad, result = lax.optimization_barrier((grad, result))
            outputs.append(result)
            layer_out = spread(outputs)
        else:
            gain_part = exchange(
                jnp.where(core == 0, gain_grads[0], gain_grads[1]),
                jnp.where(core == 0, gain_grads[1], gain_grads[0]),
            )
            gain_part = gain_part.reshape(2, 4, -1).transpose(1, 0, 2)
            gain_width = gain_part.shape[2]
            gain_part = jnp.pad(gain_part, ((0, 0), (0, 14), (0, half - gain_width)))
            input_grad = spread(input_grads)
        attn_parts[layer] = attn_part

    rows = attn_parts[0].shape[1]
    attn_pair = jnp.concatenate(
        [
            jnp.concatenate([attn_parts[0], gain_part], axis=1),
            jnp.pad(attn_parts[1], ((0, 0), (0, 16), (0, 0))),
        ],
        axis=2,
    )
    attn_pair, pair_sums[0] = lax.optimization_barrier((attn_pair, pair_sums[0]))
    attn_pair = sum_z(attn_pair)
    attn_pair, input_grad, layer_out = lax.optimization_barrier((attn_pair, input_grad, layer_out))
    total = attn_pair[rows : rows + 2, :gain_width].astype(wide)

    def to_owner(first, second):
        own = jnp.where(core == 0, first, second)
        other = swap(jnp.where(core == 0, second, first))
        both = [jnp.where(core == 0, own, other), jnp.where(core == 0, other, own)]
        return plane_gather(jnp.concatenate(both, axis=1), q)

    def split_halves(stack):
        cut = stack.shape[2] // 2
        return stack[:, :, :cut], stack[:, :, cut:]

    pair_half = split_halves(to_owner(*pair_sums))
    attn_half_sums = split_halves(to_owner(attn_pair[:rows, :half], attn_pair[:rows, half:]))

    attn_cols = jnp.concatenate(
        [part[num] for num in range(TEAM) for part in attn_half_sums], axis=1
    ).astype(wide)

    def hidden_cols(start):
        return jnp.concatenate(
            [
                part[num, :, start : start + own_hid]
                for num in range(TEAM)
                for part in pair_half
            ],
            axis=1,
        ).astype(wide)

    gate_cols, up_cols = hidden_cols(0), hidden_cols(own_hid)
    down_sum = jnp.stack(
        [unfold(part[:, :, 2 * own_hid :], width) for part in pair_half]
    ).astype(wide)
    qw, kw = w_query.shape[2], w_key.shape[2]
    return (
        layer_out,
        input_grad,
        total[0][None],
        attn_cols[None, :, :qw],
        attn_cols[None, :, qw : qw + kw],
        attn_cols[None, :, qw + kw : qw + 2 * kw],
        attn_cols[None, :, qw + 2 * kw :],
        total[1][None],
        gate_cols[None],
        up_cols[None],
        down_sum.reshape(1, -1, width),
    )


def solution(mesh):
    placed = (
        P(None, "replica", "shard", None),
        P(None, "replica", None),
        P("section", "shard"),
        P("section", "shard", None),
        P("section", "shard", None),
        P("section", "shard", None),
        P("section", "shard", None),
        P("section", "shard"),
        P("section", "shard", None),
        P("section", "shard", None),
        P("section", "shard", None),
        P(None, "replica", "shard", None),
    )
    return jax.shard_map(
        local,
        mesh=mesh,
        in_specs=placed,
        out_specs=(
            P("section", None, "replica", "shard", None),
            P("section", None, "replica", "shard", None),
            P("section", "shard"),
            P("section", "shard", None),
            P("section", "shard", None),
            P("section", "shard", None),
            P("section", "shard", None),
            P("section", "shard"),
            P("section", "shard", None),
            P("section", "shard", None),
            P("section", "shard", None),
        ),
        check_vma=False,
    )
```

```python
import jax
import jax.numpy as jnp
from jax import lax
from jax.experimental import pallas as pl
from jax.experimental.pallas import tpu as pltpu
from jax.sharding import PartitionSpec as P

QH = 15
KVH = 5
HD = 64
TEAM = 4

rope_base = 100000.0
norm_eps = 1e-05
mask_fill = -1000000000.0

low = jnp.bfloat16
wide = jnp.float32


def dot(a, b):
    return jnp.dot(a, b, preferred_element_type=wide)


def dot_t(a, b):
    return lax.dot_general(a, b, (((1,), (1,)), ((), ())), preferred_element_type=wide)


def dot_l(a, b):
    return lax.dot_general(a, b, (((0,), (0,)), ((), ())), preferred_element_type=wide)


def to_core(value, target):
    return lax.ppermute(value, "section", [(1 - target, target)])


def swap(value):
    return lax.ppermute(value, "section", [(0, 1), (1, 0)])


def z_send(value, hop, core=None):
    count = lax.axis_size("shard")
    cores = range(lax.axis_size("section")) if core is None else (core,)
    pairs = [(c * count + z, c * count + (z + hop) % count) for c in cores for z in range(count)]
    return lax.ppermute(value, ("section", "shard"), pairs)


def plane_send(value, flip, core=None):
    count = lax.axis_size("replica")
    cores = range(lax.axis_size("section")) if core is None else (core,)
    pairs = [(c * count + r, c * count + (r ^ flip)) for c in cores for r in range(count)]
    return lax.ppermute(value, ("section", "replica"), pairs)


def turn_over(value):
    count = lax.axis_size("replica")
    pairs = [
        (b * count + r, (r % TEAM) * count + r - r % TEAM + b)
        for b in range(TEAM)
        for r in range(count)
    ]
    return lax.ppermute(value, ("shard", "replica"), pairs)


def pick(stack, index):
    return lax.dynamic_index_in_dim(stack, index, 0, keepdims=False)


def place_kernel(index_ref, *refs):
    *blocks, stack, sems = refs
    copies = [
        pltpu.make_async_copy(block, stack.at[index_ref[k]], sems.at[k])
        for k, block in enumerate(blocks)
    ]
    for copy in copies:
        copy.start()
    for copy in copies:
        copy.wait()


def place(parts):
    count, block = len(parts), parts[0][1]
    shape = jax.ShapeDtypeStruct((count,) + block.shape, block.dtype)
    moved = 2 * count * block.size * block.dtype.itemsize
    return pl.pallas_call(
        place_kernel,
        out_shape=shape,
        in_specs=[pl.BlockSpec(memory_space=pltpu.SMEM)]
        + [pl.BlockSpec(memory_space=pltpu.VMEM)] * count,
        out_specs=pl.BlockSpec(memory_space=pl.ANY),
        scratch_shapes=[pltpu.SemaphoreType.DMA((count,))],
        cost_estimate=pl.CostEstimate(flops=0, bytes_accessed=moved, transcendentals=0),
        compiler_params=pltpu.CompilerParams(vmem_limit_bytes=24 * 2**20),
    )(jnp.stack([jnp.asarray(i, jnp.int32) for i, _ in parts]), *(b for _, b in parts))


def z_gather(block, z, core=None):
    return place([(z, block)] + [((z - hop) % 4, z_send(block, hop, core)) for hop in (1, 2, 3)])


def z_trade(stack, z, core=None):
    return [(z, pick(stack, z))] + [
        ((z - hop) % 4, z_send(pick(stack, (z + hop) % 4), hop, core)) for hop in (1, 2, 3)
    ]


def plane_gather(block, q, core=None):
    return place([(q, block)] + [(q ^ flip, plane_send(block, flip, core)) for flip in (1, 2, 3)])


def plane_trade(stack, q, core=None):
    return place(
        [(q, pick(stack, q))]
        + [(q ^ flip, plane_send(pick(stack, q ^ flip), flip, core)) for flip in (1, 2, 3)]
    )


def plane_sum(partial):
    half = partial.shape[0] // 2
    first, second = partial[:half].astype(low), partial[half:].astype(low)

    def both(mine, flip):
        return mine.astype(wide) + plane_send(mine, flip).astype(wide)

    first, second = both(first, 1).astype(low), both(second, 2).astype(low)
    return jnp.concatenate([both(first, 2), both(second, 1)])


def teams_sum(value):
    flip = TEAM
    while flip < lax.axis_size("replica"):
        sent = value.astype(low)
        value = sent.astype(wide) + plane_send(sent, flip).astype(wide)
        flip *= 2
    return value


def after(value, earlier):
    return lax.optimization_barrier((value, earlier))[0]


def fold(block, width):
    rows, cols = block.shape[-2], block.shape[-1]
    if cols % width == 0:
        return jnp.concatenate(
            [block[..., start : start + width] for start in range(0, cols, width)], axis=-2
        )
    tail = block[..., width:]
    tail = jnp.concatenate([tail[..., : rows // 2, :], tail[..., rows // 2 :, :]], axis=-1)
    return jnp.concatenate([block[..., :width], tail], axis=-2)


def unfold(block, cols):
    width = block.shape[-1]
    if cols % width == 0:
        rows = block.shape[-2] * width // cols
        return jnp.concatenate(
            [block[..., k * rows : (k + 1) * rows, :] for k in range(cols // width)], axis=-1
        )
    rows = block.shape[-2] * width // cols
    tail = block[..., rows:, :]
    tail = jnp.concatenate([tail[..., : width // 2], tail[..., width // 2 :]], axis=-2)
    return jnp.concatenate([block[..., :rows, :], tail], axis=-1)


def tables(segments):
    count = segments.shape[0]
    rows = jnp.arange(count, dtype=jnp.int32)
    before = jnp.sum((segments[None, :] < segments[:, None]).astype(jnp.int32), axis=1)
    allowed = (segments[None, :] == segments[:, None]) & (rows[None, :] <= rows[:, None])
    frequency = rope_base ** (-jnp.arange(HD // 2).astype(wide) * (2.0 / HD))
    angles = (rows - before).astype(wide)[:, None] * frequency[None, :]
    angles = jnp.concatenate([angles, angles], axis=1)
    return allowed, jnp.cos(angles)[:, None, :], jnp.sin(angles)[:, None, :]


def rotate_fwd(values, cos_tab, sin_tab):
    half = HD // 2
    turned = jnp.concatenate([-values[..., half:], values[..., :half]], axis=-1)
    return values * cos_tab + turned * sin_tab


def rotate_back(values, cos_tab, sin_tab):
    half = HD // 2
    shifted = values * sin_tab
    return values * cos_tab + jnp.concatenate([shifted[..., half:], -shifted[..., :half]], axis=-1)


def row_scale(values):
    return lax.rsqrt(jnp.mean(values * values, axis=-1, keepdims=True) + norm_eps)


def norm_back(grad_normed, values, gain):
    factor = row_scale(values)
    gain_grad = jnp.sum(grad_normed * values * factor, axis=0)
    weighted = grad_normed * gain
    inner = jnp.mean(weighted * values, axis=-1, keepdims=True)
    return gain_grad, factor * weighted - values * factor * factor * factor * inner


def attention_fwd(layer_in, tabs, attn_w, gain, blocks):
    allowed, cos_tab, sin_tab = tabs
    count = layer_in.shape[0]
    x = layer_in.astype(wide)
    normed = (x * row_scale(x) * gain).astype(low)
    mixed = dot(normed, attn_w[1])
    query_pre = jnp.concatenate([dot(normed, attn_w[0]), mixed[:, :320]], axis=1)
    queries = rotate_fwd(query_pre.reshape(count, QH, HD), cos_tab, sin_tab).astype(low)
    queries = queries.reshape(count, KVH, QH // KVH, HD)
    keys = rotate_fwd(mixed[:, 320:].reshape(count, KVH, HD), cos_tab, sin_tab).astype(low)
    values = dot(normed, attn_w[2][:, :320]).astype(low).reshape(count, KVH, HD)
    values, blocks = lax.optimization_barrier((values, blocks))
    scores = jnp.einsum("cgrd,sgd->grcs", queries, keys, preferred_element_type=wide) * HD**-0.5
    scores = jnp.where(allowed[None, None], scores, mask_fill)
    exponent = jnp.exp(scores - jnp.max(scores, axis=-1, keepdims=True))
    probs = exponent / jnp.sum(exponent, axis=-1, keepdims=True)
    attended = jnp.einsum("grcs,sgd->cgrd", probs.astype(low), values, preferred_element_type=wide)
    attended = attended.reshape(count, QH * HD).astype(low)
    branch = jnp.concatenate([dot(attended, attn_w[2][:, 320:]), dot(attended, attn_w[3])], axis=1)
    return x + branch, (normed, queries, keys, values, probs, attended), blocks


def attention_back(layer_in, grad_middle, tabs, attn_w, gain, kept):
    allowed, cos_tab, sin_tab = tabs
    normed, queries, keys, values, probs, attended = kept
    count = layer_in.shape[0]
    branch = grad_middle.astype(low)
    grad_att = dot_t(branch[:, :320], attn_w[2][:, 320:]) + dot_t(branch[:, 320:], attn_w[3])
    grad_att = grad_att.astype(low).reshape(count, KVH, QH // KVH, HD)
    grad_probs = jnp.einsum("cgrd,sgd->grcs", grad_att, values, preferred_element_type=wide)
    centre = jnp.sum(probs * grad_probs, axis=-1, keepdims=True)
    grad_scores = (probs * (grad_probs - centre)).astype(low)
    scale = HD**-0.5
    grad_q = jnp.einsum("grcs,sgd->cgrd", grad_scores, keys, preferred_element_type=wide) * scale
    grad_k = jnp.einsum("grcs,cgrd->sgd", grad_scores, queries, preferred_element_type=wide) * scale
    grad_v = jnp.einsum(
        "grcs,cgrd->sgd", probs.astype(low), grad_att, preferred_element_type=wide
    )
    grad_q = rotate_back(grad_q.reshape(count, QH, HD), cos_tab, sin_tab).astype(low)
    grad_k = rotate_back(grad_k, cos_tab, sin_tab).astype(low)
    pieces = [
        grad_q.reshape(count, QH * HD),
        grad_k.reshape(count, KVH * HD),
        grad_v.astype(low).reshape(count, KVH * HD),
        branch,
    ]
    right = jnp.concatenate(pieces, axis=1)
    grad_normed = (
        dot_t(right[:, :640], attn_w[0])
        + dot_t(right[:, 640:1280], attn_w[1])
        + dot_t(right[:, 1280:1600], attn_w[2][:, :320])
    )
    x = layer_in.astype(wide)
    gain_grad, through = norm_back(grad_normed, x, gain)
    return grad_middle + through, right, gain_grad


def local(
    hidden_in,
    segment_ids,
    norm_attn,
    w_query,
    w_key,
    w_value,
    w_out,
    norm_ffn,
    w_gate,
    w_up,
    w_down,
    out_grad,
):
    core = lax.axis_index("section")
    z = lax.axis_index("shard")
    replica = lax.axis_index("replica")
    q = replica % TEAM
    layers = 2
    group, width = hidden_in.shape[2], hidden_in.shape[3]

    chunk = (w_query.shape[2] * 2 + w_key.shape[2] * 2) // TEAM
    hid = w_gate.shape[2] // TEAM
    down_rows = w_down.shape[1] // TEAM
    attn_all = jnp.concatenate([w_query[0], w_key[0], w_value[0], w_out[0]], axis=1)
    attn_share = lax.dynamic_slice_in_dim(attn_all, q * chunk, chunk, axis=1)
    half, strip = chunk // 2, down_rows // 2
    own_hid = hid // 2

    def ffn_half(which):
        start = q * hid + which * own_hid
        gate, up = (
            lax.dynamic_slice_in_dim(w[0], start, own_hid, axis=1) for w in (w_gate, w_up)
        )
        down = lax.dynamic_slice_in_dim(w_down[0], which * own_hid + q * strip, strip, axis=0)
        return jnp.concatenate([gate, up, fold(down, half)], axis=1)

    ffn_low, ffn_high = ffn_half(0), ffn_half(1)
    ffn_keep = jnp.where(core == 0, ffn_low, ffn_high)
    ffn_got = swap(jnp.where(core == 0, ffn_high, ffn_low))
    ffn_shares = [jnp.where(core == layer, ffn_keep, ffn_got) for layer in range(layers)]

    def give(value, owner):
        return jnp.where(core == owner, value, to_core(value, 1 - owner))

    def both_layers(own):
        other = swap(own)
        return [jnp.where(core == layer, own, other) for layer in range(layers)]

    own_segments = lax.dynamic_slice_in_dim(pick(segment_ids[:, 0], core), z * group, group)
    marks = jnp.zeros((16, width), low)
    marks = marks.at[0, :group].set(own_segments.astype(low))
    marks = marks.at[1, : norm_attn.shape[1]].set(norm_attn[0])
    marks = marks.at[2, : norm_ffn.shape[1]].set(norm_ffn[0])
    entry = jnp.concatenate([pick(hidden_in[:, 0], core), pick(out_grad[:, 0], core), marks])
    attn_rows = z_gather(attn_share, z, 0).reshape(-1, chunk)
    attn_rows, entry, ffn_shares = lax.optimization_barrier(
        (attn_rows, turn_over(entry), ffn_shares)
    )
    entry = plane_gather(entry, q)
    turn = to_core(attn_rows[:16, :128], 1)
    hidden = entry[:, :group].reshape(-1, width)
    top_grad = entry[:, group : 2 * group].reshape(-1, width)
    entry_marks = entry[:, 2 * group :]
    segments = entry_marks[:, 0, :group].reshape(-1).astype(jnp.int32)
    tabs = tables(segments)
    own_gains = entry_marks[:, 1:3, : norm_attn.shape[1]]
    gains = both_layers(own_gains.transpose(1, 0, 2).reshape(2, -1))
    gains = [gain.astype(wide) for gain in gains]

    attn_w, ffn_w, down_w = [None] * 2, [None] * 2, [None] * 2
    rows = z_gather(after(attn_share, turn), z, 1).reshape(-1, chunk)
    blocks = [lax.all_gather(ffn_shares[0], "shard"), None]
    attn_stack, gains, blocks[0], ffn_shares[1] = lax.optimization_barrier(
        (plane_gather(attn_rows, q, 0), gains, blocks[0], ffn_shares[1])
    )
    blocks[1] = lax.all_gather(ffn_shares[1], "shard")
    attn_w[0] = give(attn_stack, 0)

    def unpack(stack):
        own = stack[:, :, : 2 * own_hid].reshape(-1, 2 * own_hid)
        down = unfold(plane_trade(stack[:, :, 2 * own_hid :], q), width).reshape(-1, width)
        return (own, swap(own)), (down, swap(down))

    attn_w[1] = give(plane_gather(after(rows, attn_w[0]), q, 1), 1)

    inputs, kept, outputs = [hidden], [], []
    for layer in range(layers):
        middle, kept_attn, ready = attention_fwd(
            inputs[layer], tabs, attn_w[layer], gains[layer][0], blocks[0] if layer == 0 else ()
        )
        if layer == 0:
            ffn_w[0], down_w[0] = unpack(ready)
        normed = (middle * row_scale(middle) * gains[layer][1]).astype(low)
        gates, ups, acts, partial = [], [], [], 0.0
        for weights, down in zip(ffn_w[layer], down_w[layer]):
            both = dot(normed, weights)
            gate, up = both[:, :own_hid], both[:, own_hid:]
            act = (gate * jax.nn.sigmoid(gate) * up).astype(low)
            partial = partial + dot(act, down)
            gates.append(gate)
            ups.append(up)
            acts.append(act)
        kept.append((kept_attn, middle, normed, gates, ups, acts))
        if layer < layers - 1:
            result = (middle + plane_sum(partial)).astype(low)
            result, second = lax.optimization_barrier((result, blocks[1]))
            ffn_w[1], down_w[1] = unpack(second)
            outputs.append(result)
            inputs.append(result)

    def spread(by_layer):
        mine = jnp.where(core == 0, by_layer[0], by_layer[1])
        other = swap(jnp.where(core == 0, by_layer[1], by_layer[0]))
        stack = jnp.where(
            core == 0, jnp.stack([mine, other]), jnp.stack([other, mine])
        ).reshape(2, 4, group, width)
        return turn_over(lax.dynamic_index_in_dim(stack, q, 1, keepdims=False))[None, :, None]

    def exchange(mine, other):
        return (mine + swap(other.astype(low)).astype(wide)).astype(low)

    def sum_z(stack):
        total = lax.psum_scatter(stack, "shard", scatter_dimension=0, tiled=False)
        return teams_sum(total.astype(wide)).astype(low)

    split = w_query.shape[2] + w_key.shape[2] * 2

    def gather_halves(own, owner):
        other = to_core(own, owner)
        return jnp.concatenate([own, other] if owner == 0 else [other, own], axis=1)

    def attn_half(kept_attn, right, which):
        start = q * chunk + which * half
        part = lax.dynamic_slice_in_dim(right, start, half, axis=1)
        column = start + jnp.arange(half)
        return jnp.where(
            column[None, :] < split, dot_l(kept_attn[0], part), dot_l(kept_attn[5], part)
        )

    gain_grads, input_grads = [None] * 2, [None] * 2
    attn_parts, pair_sums = [None] * 2, [None] * 2
    grad = top_grad
    for layer in reversed(range(layers)):
        kept_attn, middle, normed, gates, ups, acts = kept[layer]
        down_part = exchange(*(dot_l(act, grad) for act in acts))
        down_part = plane_trade(down_part.reshape(TEAM, strip, width), q)
        sides, grad_partial = [], 0.0
        for side in (0, 1):
            gate, up = gates[side], ups[side]
            grad_act = dot_t(grad, down_w[layer][side])
            sig = jax.nn.sigmoid(gate)
            grad_gate = (grad_act * up * sig * (1.0 + gate * (1.0 - sig))).astype(low)
            grad_up = (grad_act * gate * sig).astype(low)
            sides.append(jnp.concatenate([grad_gate, grad_up], axis=1))
            grad_partial = grad_partial + dot_t(sides[side], ffn_w[layer][side])
        grad_normed = plane_sum(grad_partial)
        ffn_part = exchange(*(dot_l(normed, part) for part in sides))
        pair = jnp.concatenate(
            [ffn_part.reshape(4, -1, 2 * own_hid), fold(down_part, half)], axis=2
        )
        grad_normed, pair = lax.optimization_barrier((grad_normed, pair))
        if layer == 0:
            grad_normed, pair, pair_sums[1] = lax.optimization_barrier(
                (grad_normed, pair, pair_sums[1])
            )
        pair_sums[layer] = sum_z(pair)
        gain_ffn, through = norm_back(grad_normed, middle, gains[layer][1])
        grad_middle = grad.astype(wide) + through
        grad_in, right, gain_attn = attention_back(
            inputs[layer], grad_middle, tabs, attn_w[layer], gains[layer][0], kept_attn
        )
        grad = grad_in.astype(low)
        gain_grads[layer] = jnp.stack([gain_attn, gain_ffn])
        input_grads[layer] = grad
        attn_part = exchange(
            attn_half(kept_attn, right, core), attn_half(kept_attn, right, 1 - core)
        ).reshape(4, -1, half)
        if layer == 1:
            result = (middle + plane_sum(after(partial, grad_normed))).astype(low)
            grad, result = lax.optimization_barrier((grad, result))
            outputs.append(result)
            layer_out = spread(outputs)
        else:
            gain_part = exchange(
                jnp.where(core == 0, gain_grads[0], gain_grads[1]),
                jnp.where(core == 0, gain_grads[1], gain_grads[0]),
            )
            gain_part = gain_part.reshape(2, 4, -1).transpose(1, 0, 2)
            gain_width = gain_part.shape[2]
            gain_part = jnp.pad(gain_part, ((0, 0), (0, 14), (0, half - gain_width)))
            input_grad = spread(input_grads)
        attn_parts[layer] = attn_part

    rows = attn_parts[0].shape[1]
    attn_pair = jnp.concatenate(
        [
            jnp.concatenate([attn_parts[0], gain_part], axis=1),
            jnp.pad(attn_parts[1], ((0, 0), (0, 16), (0, 0))),
        ],
        axis=2,
    )
    whole_1 = plane_gather(gather_halves(pair_sums[1], 1), q, 1)
    attn_pair, pair_sums[0], whole_1 = lax.optimization_barrier((attn_pair, pair_sums[0], whole_1))
    attn_pair = sum_z(attn_pair)
    attn_pair, input_grad, layer_out = lax.optimization_barrier((attn_pair, input_grad, layer_out))
    total = attn_pair[rows : rows + 2, :gain_width].astype(wide)

    def to_owner(first, second):
        own = jnp.where(core == 0, first, second)
        other = swap(jnp.where(core == 0, second, first))
        both = [jnp.where(core == 0, own, other), jnp.where(core == 0, other, own)]
        return plane_gather(jnp.concatenate(both, axis=1), q)

    def split_halves(stack):
        cut = stack.shape[2] // 2
        return stack[:, :, :cut], stack[:, :, cut:]

    whole_0 = plane_gather(gather_halves(pair_sums[0], 0), q, 0)
    pair_half = split_halves(jnp.where(core == 0, whole_0, whole_1))
    attn_half_sums = split_halves(to_owner(attn_pair[:rows, :half], attn_pair[:rows, half:]))

    attn_cols = jnp.concatenate(
        [part[num] for num in range(TEAM) for part in attn_half_sums], axis=1
    ).astype(wide)

    def hidden_cols(start):
        return jnp.concatenate(
            [
                part[num, :, start : start + own_hid]
                for num in range(TEAM)
                for part in pair_half
            ],
            axis=1,
        ).astype(wide)

    gate_cols, up_cols = hidden_cols(0), hidden_cols(own_hid)
    down_sum = jnp.stack(
        [unfold(part[:, :, 2 * own_hid :], width) for part in pair_half]
    ).astype(wide)
    qw, kw = w_query.shape[2], w_key.shape[2]
    return (
        layer_out,
        input_grad,
        total[0][None],
        attn_cols[None, :, :qw],
        attn_cols[None, :, qw : qw + kw],
        attn_cols[None, :, qw + kw : qw + 2 * kw],
        attn_cols[None, :, qw + 2 * kw :],
        total[1][None],
        gate_cols[None],
        up_cols[None],
        down_sum.reshape(1, -1, width),
    )


def solution(mesh):
    placed = (
        P(None, "replica", "shard", None),
        P(None, "replica", None),
        P("section", "shard"),
        P("section", "shard", None),
        P("section", "shard", None),
        P("section", "shard", None),
        P("section", "shard", None),
        P("section", "shard"),
        P("section", "shard", None),
        P("section", "shard", None),
        P("section", "shard", None),
        P(None, "replica", "shard", None),
    )
    return jax.shard_map(
        local,
        mesh=mesh,
        in_specs=placed,
        out_specs=(
            P("section", None, "replica", "shard", None),
            P("section", None, "replica", "shard", None),
            P("section", "shard"),
            P("section", "shard", None),
            P("section", "shard", None),
            P("section", "shard", None),
            P("section", "shard", None),
            P("section", "shard"),
            P("section", "shard", None),
            P("section", "shard", None),
            P("section", "shard", None),
        ),
        check_vma=False,
    )
```
